32 devices in a mesh: groups: 2 (over y), ctx: 4 (over z), ch: 4 (over x, core).
Axes of the slice: x: 2, y: 2, z: 4, core: 2. Of those that a mesh axis runs over, the one named last changes fastest.
Arguments:
- projections: bfloat16 [1024, 3, 4096], P(('groups', 'ctx'), None, 'ch'), parts along dimension 0, may hold values from -6 to 6
- short_taps: float32 [3, 3, 4096], P(None, None, 'ch'), may hold values from -3 to 3
- residues: float32 [4096, 16], P(('ch', 'ctx')), may hold values from -2 to 2
- decay_rates: float32 [4096, 16], P(('ch', 'ctx')), may hold values from 0.25 to 16
- skip_gain: float32 [4096], P(('ch', 'ctx')), may hold values from -3 to 3
- grad_mixed: bfloat16 [1024, 2048], P(('groups', 'ctx'), 'ch'), parts along dimension 0, may hold values from -6 to 6
- out_weight: bfloat16 [4096, 2048], P('ch', 'ctx'), may hold values from -0.09375 to 0.09375
Outputs:
- grad_projections: bfloat16 [1024, 3, 4096], P(('groups', 'ctx'), None, 'ch'), parts along dimension 0
- grad_short: float32 [6, 3, 4096], P('groups', None, 'ch'), parts along dimension 0
- grad_skip: float32 [8192], P(('groups', 'ch', 'ctx')), parts along dimension 0
- grad_residues: float32 [8192, 16], P(('groups', 'ch', 'ctx')), parts along dimension 0
- grad_log_rates: float32 [8192, 16], P(('groups', 'ch', 'ctx')), parts along dimension 0
- grad_weight: float32 [8192, 2048], P(('groups', 'ch'), 'ctx'), parts along dimension 0
The draws below stay inside these ranges and needn't reach their ends.
There are 2 independent parts, one for each index of `groups`. The reference program is written for one: setup_inputs(seed, part) draws one part's arguments, and reference() takes and returns one part's arrays. A program takes and returns all parts, laid end to end along the dimension named above; an argument that names none is the same for every part. Nothing has to cross between parts.
All inputs are finite; a program needn't handle non-finite values.
Results may differ from the reference program's by a relative error of at most 0.006.
Values may be sent and summed in bfloat16 or wider, within the bound.
A program may use at most 64 MiB of HBM per device.

```python
import math
from functools import partial
import jax
import jax.numpy as jnp
from jax import lax

CHANNELS = 4096
OUT_WIDTH = 2048
SHORT = 3
ORDER = 16
SEQ = 512


def level_of(own_key, extent, cuts, least, high):
    gain = 1.0
    for dim, shards_of in cuts:
        steps = jax.random.uniform(jax.random.fold_in(jax.random.fold_in(own_key, 6), dim), (shards_of,), jnp.float32, least / len(cuts), high / len(cuts))
        gain = gain * jnp.repeat(jnp.exp(steps), extent[dim] // shards_of).reshape((-1,) + (1,) * (len(extent) - 1 - dim))
    return gain


def normal_values(key, extent, deviation, limit, cuts=(), kind=jnp.bfloat16):
    array = deviation * jax.random.normal(key, extent, jnp.float32)
    if cuts:
        array = array * level_of(key, extent, cuts, -0.22, 0.18)
    return jnp.clip(array, -limit, limit).astype(kind)


def setup_inputs(seed: int = 0, part: int = 0) -> dict:
    streams_of = jax.random.split(jax.random.key(seed), 8)
    own_keys = jax.random.split(jax.random.fold_in(streams_of[7], part), 8)
    projections = normal_values(own_keys[0], (SEQ, 3, CHANNELS), 1.0, 6.0, ((0, 4), (2, 4)))
    short_taps = normal_values(streams_of[1], (SHORT, 3, CHANNELS), 0.5, 3.0, ((2, 4),), jnp.float32)
    residues = normal_values(streams_of[2], (CHANNELS, ORDER), 0.3, 2.0, ((0, 16),), jnp.float32)
    decay_rates = jnp.clip(jnp.exp(math.log(16.0) - 4.158883 * jax.random.uniform(streams_of[3], (CHANNELS, ORDER), jnp.float32) ** level_of(streams_of[3], (CHANNELS, ORDER), ((0, 16),), -0.2, 0.2)), 0.25, 16.0)
    skip_gain = normal_values(streams_of[4], (CHANNELS,), 0.5, 3.0, ((0, 16),), jnp.float32)
    grad_mixed = normal_values(own_keys[5], (SEQ, OUT_WIDTH), 1.0, 6.0, ((0, 4), (1, 4)))
    out_weight = normal_values(streams_of[6], (CHANNELS, OUT_WIDTH), CHANNELS ** -0.5, 0.09375, ((0, 4), (1, 4)))
    return dict(projections=projections, short_taps=short_taps, residues=residues, decay_rates=decay_rates, skip_gain=skip_gain, grad_mixed=grad_mixed, out_weight=out_weight)


def make_filter(residues, decay_rates, seq_len):
    positions = jnp.arange(seq_len, dtype=jnp.float32) / seq_len
    amplitude = residues * jnp.sqrt(2.0 * decay_rates / seq_len)
    basis = jnp.exp(-decay_rates[:, :, None] * positions[None, None, :])
    return jnp.einsum('cn,cnt->ct', amplitude, basis, precision=lax.Precision.HIGHEST)

def reference(projections, short_taps, residues, decay_rates, skip_gain, grad_mixed, out_weight):
    seq_len = projections.shape[0]
    norm_factor = math.sqrt(seq_len)
    padded_in = jnp.pad(projections.astype(jnp.float32), ((SHORT - 1, 0), (0, 0), (0, 0)))
    mixed_in = jnp.zeros(projections.shape, jnp.float32)
    for lag_index in range(SHORT):
        start_row = SHORT - 1 - lag_index
        mixed_in = mixed_in + short_taps[lag_index] * padded_in[start_row:start_row + seq_len]
    query_rows = mixed_in[:, 0]
    key_rows = mixed_in[:, 1]
    value_rows = mixed_in[:, 2]
    gated_rows = (key_rows * value_rows).astype(jnp.bfloat16)
    grad_out = jnp.dot(grad_mixed, out_weight.T, preferred_element_type=jnp.float32)
    grad_y = (grad_out * query_rows).astype(jnp.bfloat16)
    width = 256
    count = CHANNELS // width
    length = 2 * seq_len

    def long_block(inputs):
        res_blk, rate_blk, gain_blk, gate_blk, grad_blk = inputs
        long_filter, filter_vjp = jax.vjp(partial(make_filter, seq_len=seq_len), res_blk, rate_blk)
        gate_f = gate_blk.astype(jnp.float32)
        grad_f = grad_blk.astype(jnp.float32)
        spec_h = jnp.fft.rfft(long_filter, n=length)
        spec_u = jnp.fft.rfft(gate_f, n=length)
        spec_g = jnp.fft.rfft(grad_f, n=length)
        mix_cols = (jnp.fft.irfft(spec_h * spec_u, n=length)[:, :seq_len] + gain_blk[:, None] * gate_f).astype(jnp.bfloat16)
        grad_cols = (jnp.fft.irfft(jnp.conj(spec_h) * spec_g, n=length)[:, :seq_len] + gain_blk[:, None] * grad_f).astype(jnp.bfloat16)
        grad_filter = jnp.fft.irfft(spec_g * jnp.conj(spec_u), n=length)[:, :seq_len].astype(jnp.float32)
        grad_res, grad_rate = filter_vjp(grad_filter)
        skip_sum = lax.optimization_barrier(jnp.sum(grad_f * gate_f, axis=1))
        return (mix_cols, grad_cols, grad_res / norm_factor, grad_rate * rate_blk / norm_factor, skip_sum / norm_factor)
    mix_b, grad_b, res_b, rate_b, skip_b = lax.map(long_block, (residues.reshape(count, width, ORDER), decay_rates.reshape(count, width, ORDER), skip_gain.reshape(count, width), gated_rows.T.reshape(count, width, seq_len), grad_y.T.reshape(count, width, seq_len)))
    mix_rows = mix_b.reshape(CHANNELS, seq_len).T
    grad_gated = grad_b.reshape(CHANNELS, seq_len).T
    grad_residues = res_b.reshape(CHANNELS, ORDER)
    grad_log_rates = rate_b.reshape(CHANNELS, ORDER)
    grad_skip = skip_b.reshape(CHANNELS)
    mixed_out = (query_rows * mix_rows).astype(jnp.bfloat16)
    grad_mix = jnp.stack([grad_out * mix_rows, grad_gated * value_rows, grad_gated * key_rows], axis=1)
    padded_grad = jnp.pad(grad_mix, ((0, SHORT - 1), (0, 0), (0, 0)))
    running = jnp.zeros(grad_mix.shape, jnp.float32)
    short_terms = []
    for lag_index in range(SHORT):
        running = running + short_taps[lag_index] * padded_grad[lag_index:lag_index + seq_len]
        start_row = SHORT - 1 - lag_index
        short_terms.append(lax.optimization_barrier(jnp.sum(grad_mix * padded_in[start_row:start_row + seq_len], axis=0)))
    grad_projections = running.astype(jnp.bfloat16)
    grad_short = jnp.stack(short_terms, axis=0) / norm_factor
    grad_weight = jnp.dot(mixed_out.T, grad_mixed, preferred_element_type=jnp.float32) / norm_factor
    return (grad_projections, grad_short, grad_skip, grad_residues, grad_log_rates, grad_weight)
```

```python
from functools import partial
import math

import jax
import jax.numpy as jnp
import numpy as np
from jax import lax
from jax.sharding import PartitionSpec as P

SHORT = 3


def from_behind(x, axis, by):
    peers = lax.axis_size(axis)
    pairs = [(i, i + by) for i in range(peers) if 0 <= i + by < peers]
    return lax.ppermute(x, axis, pairs)


def make_filter(residues, decay_rates, seq_len):
    positions = jnp.arange(seq_len, dtype=jnp.float32) / seq_len
    amplitude = residues * jnp.sqrt(2.0 * decay_rates / seq_len)
    basis = jnp.exp(-decay_rates[:, :, None] * positions[None, None, :])
    return jnp.einsum("cn,cnt->ct", amplitude, basis, precision=lax.Precision.HIGHEST)


def circle(rows_count, cols_count, period):
    left_idx = jnp.arange(rows_count, dtype=jnp.int32)[:, None]
    right_idx = jnp.arange(cols_count, dtype=jnp.int32)[None, :]
    angle = (left_idx * right_idx % period).astype(jnp.float32) * (2.0 * math.pi / period)
    return (jnp.cos(angle), jnp.sin(angle))


def spectral_tables(length):
    factor_a = 1
    while factor_a * factor_a * 4 <= length and length % (factor_a * 2) == 0:
        factor_a = factor_a * 2
    factor_b = length // factor_a
    a_cos, a_sin = circle(factor_a, factor_a, factor_a)
    b_cos, b_sin = circle(factor_b, factor_b, factor_b)
    t_cos, t_sin = circle(factor_a, factor_b, length)
    return (length, factor_a, factor_b, a_cos, a_sin, b_cos, b_sin, t_cos, t_sin)


def forward_dft(signal, tables):
    length, factor_a, factor_b, a_cos, a_sin, b_cos, b_sin, t_cos, t_sin = tables
    highest = lax.Precision.HIGHEST
    channels, seq_len = signal.shape
    grid = jnp.pad(signal, ((0, 0), (0, length - seq_len))).reshape(channels, factor_a, factor_b)
    part_real = jnp.einsum("ka,cab->ckb", a_cos, grid, precision=highest)
    part_imag = -jnp.einsum("ka,cab->ckb", a_sin, grid, precision=highest)
    turn_real = part_real * t_cos + part_imag * t_sin
    turn_imag = part_imag * t_cos - part_real * t_sin
    out_real = jnp.einsum("ckb,bm->ckm", turn_real, b_cos, precision=highest) + jnp.einsum(
        "ckb,bm->ckm", turn_imag, b_sin, precision=highest
    )
    out_imag = jnp.einsum("ckb,bm->ckm", turn_imag, b_cos, precision=highest) - jnp.einsum(
        "ckb,bm->ckm", turn_real, b_sin, precision=highest
    )
    return (out_real, out_imag)


def inverse_dft(spec_real, spec_imag, seq_len, tables):
    length, factor_a, factor_b, a_cos, a_sin, b_cos, b_sin, t_cos, t_sin = tables
    highest = lax.Precision.HIGHEST
    channels = spec_real.shape[0]
    mid_real = jnp.einsum("ckm,mb->ckb", spec_real, b_cos, precision=highest) - jnp.einsum(
        "ckm,mb->ckb", spec_imag, b_sin, precision=highest
    )
    mid_imag = jnp.einsum("ckm,mb->ckb", spec_imag, b_cos, precision=highest) + jnp.einsum(
        "ckm,mb->ckb", spec_real, b_sin, precision=highest
    )
    turn_real = mid_real * t_cos - mid_imag * t_sin
    turn_imag = mid_imag * t_cos + mid_real * t_sin
    values = jnp.einsum("ak,ckb->cab", a_cos, turn_real, precision=highest) - jnp.einsum(
        "ak,ckb->cab", a_sin, turn_imag, precision=highest
    )
    return values.reshape(channels, length)[:, :seq_len] / length


def short_mix(extended, short_taps, tokens):
    running = jnp.zeros((tokens,) + extended.shape[1:], jnp.float32)
    for lag_index in range(SHORT):
        start_row = SHORT - 1 - lag_index
        running = running + short_taps[lag_index] * extended[start_row : start_row + tokens]
    return running


def mix_long(gate_cols, spec_h, gain, seq_len, tables):
    gate_f = gate_cols.astype(jnp.float32)
    u_real, u_imag = forward_dft(gate_f, tables)
    prod_real = spec_h[0] * u_real - spec_h[1] * u_imag
    prod_imag = spec_h[0] * u_imag + spec_h[1] * u_real
    mix_cols = (inverse_dft(prod_real, prod_imag, seq_len, tables) + gain[:, None] * gate_f).astype(
        jnp.bfloat16
    )
    return (mix_cols, (u_real, u_imag))


def grad_long(grad_cols_in, gate_cols, spec_u, spec_h, gain, seq_len, tables):
    grad_f = grad_cols_in.astype(jnp.float32)
    g_real, g_imag = forward_dft(grad_f, tables)
    back_real = spec_h[0] * g_real + spec_h[1] * g_imag
    back_imag = spec_h[0] * g_imag - spec_h[1] * g_real
    grad_cols = (
        inverse_dft(back_real, back_imag, seq_len, tables) + gain[:, None] * grad_f
    ).astype(jnp.bfloat16)
    corr_real = g_real * spec_u[0] + g_imag * spec_u[1]
    corr_imag = g_imag * spec_u[0] - g_real * spec_u[1]
    grad_filter = inverse_dft(corr_real, corr_imag, seq_len, tables)
    skip_sum = jnp.sum(grad_f * gate_cols.astype(jnp.float32), axis=1)
    return (grad_cols, grad_filter, skip_sum)


def body_factored(projections, short_taps, residues, decay_rates, skip_gain, grad_mixed, out_weight):
    tokens = projections.shape[0]
    seq_len = tokens * lax.axis_size("ctx")
    norm_factor = math.sqrt(seq_len)
    tables = spectral_tables(2 * seq_len)
    earlier = from_behind(projections[tokens - SHORT + 1 :], "ctx", 1)
    ext_proj = jnp.concatenate([earlier, projections], axis=0)
    mixed_in = short_mix(ext_proj, short_taps, tokens)
    query_rows = mixed_in[:, 0]
    key_rows = mixed_in[:, 1]
    value_rows = mixed_in[:, 2]
    gated_rows = (key_rows * value_rows).astype(jnp.bfloat16)
    long_filter, filter_vjp = jax.vjp(partial(make_filter, seq_len=seq_len), residues, decay_rates)
    spec_h = forward_dft(long_filter, tables)
    out_rows = lax.all_gather(grad_mixed, "ch", axis=1, tiled=True)
    grad_out = lax.dot_general(
        out_rows,
        lax.all_gather(out_weight, "ctx", axis=1, tiled=True),
        (((1,), (1,)), ((), ())),
        preferred_element_type=jnp.float32,
    )
    grad_y = (grad_out * query_rows).astype(jnp.bfloat16)
    gate_cols, grad_cols_in = (
        lax.all_to_all(gated_rows.T, "ctx", split_axis=0, concat_axis=1, tiled=True),
        lax.all_to_all(grad_y.T, "ctx", split_axis=0, concat_axis=1, tiled=True),
    )
    mix_cols, spec_u = mix_long(gate_cols, spec_h, skip_gain, seq_len, tables)
    grad_cols, grad_filter, skip_sum = grad_long(
        grad_cols_in, gate_cols, spec_u, spec_h, skip_gain, seq_len, tables
    )
    returned = (
        lax.all_to_all(mix_cols, "ctx", split_axis=1, concat_axis=0, tiled=True),
        lax.all_to_all(grad_cols, "ctx", split_axis=1, concat_axis=0, tiled=True),
    )
    mix_rows = returned[0].T
    grad_gated = returned[1].T
    grad_res, grad_rate = filter_vjp(grad_filter)
    grad_residues = grad_res / norm_factor
    grad_log_rates = grad_rate * decay_rates / norm_factor
    grad_skip = skip_sum / norm_factor
    mixed_out = (query_rows * mix_rows).astype(jnp.bfloat16)
    grad_mix = jnp.stack(
        [grad_out * mix_rows, grad_gated * value_rows, grad_gated * key_rows], axis=1
    )
    later = from_behind(grad_mix[: SHORT - 1], "ctx", -1)
    ext_grad = jnp.concatenate([grad_mix, later], axis=0)
    running = jnp.zeros(grad_mix.shape, jnp.float32)
    short_terms = []
    for lag_index in range(SHORT):
        running = running + short_taps[lag_index] * ext_grad[lag_index : lag_index + tokens]
        start_row = SHORT - 1 - lag_index
        short_terms.append(jnp.sum(grad_mix * ext_proj[start_row : start_row + tokens], axis=0))
    grad_projections = running.astype(jnp.bfloat16)
    grad_short = lax.psum(jnp.stack(short_terms, axis=0), "ctx") / norm_factor
    partial_term = lax.dot_general(
        mixed_out, out_rows, (((0,), (0,)), ((), ())), preferred_element_type=jnp.float32
    )
    weight_sum = lax.psum_scatter(partial_term, "ctx", scatter_dimension=1, tiled=True)
    grad_weight = weight_sum / norm_factor
    return (grad_projections, grad_short, grad_skip, grad_residues, grad_log_rates, grad_weight)


def wave_tables(seq_len):
    fine = 16
    steps = np.arange(seq_len, dtype=np.int64)[None, :]
    coarse = np.arange(seq_len // fine, dtype=np.int64)[:, None] * (2 * fine)
    inner = np.arange(fine, dtype=np.int64)[:, None] * 2 + 1
    outs = []
    for rows in (coarse, inner):
        angle = (rows * steps % (4 * seq_len)) * (2.0 * math.pi / (4 * seq_len))
        outs += [np.cos(angle).astype(np.float32), np.sin(angle).astype(np.float32)]
    return outs


def waves(tables):
    ca, sa, cb, sb = tables
    ca, sa = ca[:, None, :], sa[:, None, :]
    cb, sb = cb[None], sb[None]
    seq_len = ca.shape[-1]
    cos = (ca * cb - sa * sb).reshape(seq_len, seq_len)
    sin = (sa * cb + ca * sb).reshape(seq_len, seq_len)
    return jnp.concatenate([cos, sin], axis=0)


def dot0(a, b):
    return lax.dot_general(a, b, (((0,), (0,)), ((), ())), preferred_element_type=jnp.float32)


def dot1(a, b):
    return lax.dot_general(a, b, (((1,), (0,)), ((), ())), preferred_element_type=jnp.float32)


def split(x):
    high = x.astype(jnp.bfloat16)
    return high, (x - high.astype(jnp.float32)).astype(jnp.bfloat16)


def shift_down(x, by):
    return jnp.pad(x, ((by, 0), (0, 0)))[: x.shape[0]] if by else x


def shift_up(x, by):
    return jnp.pad(x, ((0, by), (0, 0)))[by:] if by else x


def body(projections, short_taps, residues, decay_rates, skip_gain, grad_mixed, out_weight):
    tokens, _, width = projections.shape
    peers = lax.axis_size("ctx")
    seq_len = tokens * peers
    if seq_len > 1024:
        return body_factored(
            projections, short_taps, residues, decay_rates, skip_gain, grad_mixed, out_weight
        )
    cols = width // peers
    me = lax.axis_index("ctx")
    norm = math.sqrt(seq_len)
    f32, bf16 = jnp.float32, jnp.bfloat16
    proj = lax.all_to_all(
        projections.transpose(1, 0, 2), "ctx", split_axis=2, concat_axis=1, tiled=True
    )
    weight = lax.all_to_all(out_weight, "ctx", split_axis=0, concat_axis=1, tiled=True)
    gm = lax.all_gather(grad_mixed, "ch", axis=1, tiled=True)
    gm = lax.all_gather(gm, "ctx", axis=0, tiled=True)
    taps = lax.dynamic_slice_in_dim(short_taps, me * cols, cols, 2)
    tables = lax.optimization_barrier([jnp.asarray(t) for t in wave_tables(seq_len)])
    wave_h, wave_l = split(waves(tables))
    rate = decay_rates.T
    amp = jnp.sqrt(2.0 * rate / seq_len)
    where = jnp.arange(seq_len, dtype=f32) / seq_len
    filt = jnp.sum((residues.T * amp)[:, None, :] * jnp.exp(-rate[:, None, :] * where[None, :, None]), axis=0)

    def forward_exact(x):
        return dot1(wave_h, x) + dot1(wave_l, x)

    def forward(x):
        high, low = split(x)
        return dot1(wave_h, high) + dot1(wave_l, high) + dot1(wave_h, low)

    def backward(top, bottom):
        high, low = split(jnp.concatenate([top, bottom], axis=0))
        return (dot0(wave_h, high) + dot0(wave_l, high) + dot0(wave_h, low)) * (1.0 / seq_len)

    def halves(x):
        return x[:seq_len], x[seq_len:]

    p, q = halves(forward(filt))
    proj_f = [proj[g].astype(f32) for g in range(3)]
    query, key, value = (
        sum(taps[j, g][None] * shift_down(proj_f[g], j) for j in range(SHORT)) for g in range(3)
    )
    gated = (key * value).astype(bf16)
    a, b = halves(forward_exact(gated))
    gated_f = gated.astype(f32)
    gain = skip_gain[None]
    mix = (backward(p * a - q * b, p * b + q * a) + gain * gated_f).astype(bf16).astype(f32)
    mixed_out = (query * mix).astype(bf16)
    mixed_all = lax.all_gather(mixed_out, "ctx", axis=1, tiled=True)

    grad_out = lax.dot_general(gm, weight, (((1,), (1,)), ((), ())), preferred_element_type=f32)
    grad_y = (grad_out * query).astype(bf16)
    grad_yf = grad_y.astype(f32)
    d, e = halves(forward_exact(grad_y))
    grad_gated = (backward(p * d + q * e, p * e - q * d) + gain * grad_yf).astype(bf16).astype(f32)
    grad_filter = backward(d * a + e * b, e * a - d * b)
    grad_skip = jnp.sum(grad_yf * gated_f, axis=0) / norm
    basis = jnp.exp(-rate[:, None, :] * where[None, :, None]) * grad_filter[None]
    moment0 = jnp.sum(basis, axis=1)
    moment1 = jnp.sum(basis * where[None, :, None], axis=1)
    grad_residues = (amp * moment0 / norm).T
    grad_log_rates = (residues.T * amp * (0.5 * moment0 - rate * moment1) / norm).T
    grad_mix = [grad_out * mix, grad_gated * value, grad_gated * key]
    grad_proj = jnp.stack(
        [
            sum(taps[j, g][None] * shift_up(grad_mix[g], j) for j in range(SHORT)).astype(bf16)
            for g in range(3)
        ]
    )
    grad_projections = lax.all_to_all(
        grad_proj, "ctx", split_axis=1, concat_axis=2, tiled=True
    ).transpose(1, 0, 2)
    short = jnp.stack(
        [
            jnp.stack([jnp.sum(grad_mix[g] * shift_down(proj_f[g], j), axis=0) for g in range(3)])
            for j in range(SHORT)
        ]
    )
    grad_short = lax.all_gather(short / norm, "ctx", axis=2, tiled=True)
    gm_own = lax.dynamic_slice_in_dim(gm, me * (gm.shape[1] // peers), gm.shape[1] // peers, 1)
    grad_weight = dot0(mixed_all, gm_own) / norm
    return (grad_projections, grad_short, grad_skip, grad_residues, grad_log_rates, grad_weight)


def solution(mesh):
    return jax.shard_map(
        body,
        mesh=mesh,
        in_specs=(
            P(("groups", "ctx"), None, "ch"),
            P(None, None, "ch"),
            P(("ch", "ctx"), None),
            P(("ch", "ctx"), None),
            P(("ch", "ctx")),
            P(("groups", "ctx"), "ch"),
            P("ch", "ctx"),
        ),
        out_specs=(
            P(("groups", "ctx"), None, "ch"),
            P("groups", None, "ch"),
            P(("groups", "ch", "ctx")),
            P(("groups", "ch", "ctx"), None),
            P(("groups", "ch", "ctx"), None),
            P(("groups", "ch"), "ctx"),
        ),
        check_vma=False,
    )
```

```python
from functools import partial
import math

import jax
import jax.numpy as jnp
import numpy as np
from jax import lax
from jax.experimental import pallas as pl
from jax.experimental.pallas import tpu as pltpu
from jax.sharding import PartitionSpec as P

SHORT = 3


def from_behind(x, axis, by):
    peers = lax.axis_size(axis)
    pairs = [(i, i + by) for i in range(peers) if 0 <= i + by < peers]
    return lax.ppermute(x, axis, pairs)


def make_filter(residues, decay_rates, seq_len):
    positions = jnp.arange(seq_len, dtype=jnp.float32) / seq_len
    amplitude = residues * jnp.sqrt(2.0 * decay_rates / seq_len)
    basis = jnp.exp(-decay_rates[:, :, None] * positions[None, None, :])
    return jnp.einsum("cn,cnt->ct", amplitude, basis, precision=lax.Precision.HIGHEST)


def circle(rows_count, cols_count, period):
    left_idx = jnp.arange(rows_count, dtype=jnp.int32)[:, None]
    right_idx = jnp.arange(cols_count, dtype=jnp.int32)[None, :]
    angle = (left_idx * right_idx % period).astype(jnp.float32) * (2.0 * math.pi / period)
    return (jnp.cos(angle), jnp.sin(angle))


def spectral_tables(length):
    factor_a = 1
    while factor_a * factor_a * 4 <= length and length % (factor_a * 2) == 0:
        factor_a = factor_a * 2
    factor_b = length // factor_a
    a_cos, a_sin = circle(factor_a, factor_a, factor_a)
    b_cos, b_sin = circle(factor_b, factor_b, factor_b)
    t_cos, t_sin = circle(factor_a, factor_b, length)
    return (length, factor_a, factor_b, a_cos, a_sin, b_cos, b_sin, t_cos, t_sin)


def forward_dft(signal, tables):
    length, factor_a, factor_b, a_cos, a_sin, b_cos, b_sin, t_cos, t_sin = tables
    highest = lax.Precision.HIGHEST
    channels, seq_len = signal.shape
    grid = jnp.pad(signal, ((0, 0), (0, length - seq_len))).reshape(channels, factor_a, factor_b)
    part_real = jnp.einsum("ka,cab->ckb", a_cos, grid, precision=highest)
    part_imag = -jnp.einsum("ka,cab->ckb", a_sin, grid, precision=highest)
    turn_real = part_real * t_cos + part_imag * t_sin
    turn_imag = part_imag * t_cos - part_real * t_sin
    out_real = jnp.einsum("ckb,bm->ckm", turn_real, b_cos, precision=highest) + jnp.einsum(
        "ckb,bm->ckm", turn_imag, b_sin, precision=highest
    )
    out_imag = jnp.einsum("ckb,bm->ckm", turn_imag, b_cos, precision=highest) - jnp.einsum(
        "ckb,bm->ckm", turn_real, b_sin, precision=highest
    )
    return (out_real, out_imag)


def inverse_dft(spec_real, spec_imag, seq_len, tables):
    length, factor_a, factor_b, a_cos, a_sin, b_cos, b_sin, t_cos, t_sin = tables
    highest = lax.Precision.HIGHEST
    channels = spec_real.shape[0]
    mid_real = jnp.einsum("ckm,mb->ckb", spec_real, b_cos, precision=highest) - jnp.einsum(
        "ckm,mb->ckb", spec_imag, b_sin, precision=highest
    )
    mid_imag = jnp.einsum("ckm,mb->ckb", spec_imag, b_cos, precision=highest) + jnp.einsum(
        "ckm,mb->ckb", spec_real, b_sin, precision=highest
    )
    turn_real = mid_real * t_cos - mid_imag * t_sin
    turn_imag = mid_imag * t_cos + mid_real * t_sin
    values = jnp.einsum("ak,ckb->cab", a_cos, turn_real, precision=highest) - jnp.einsum(
        "ak,ckb->cab", a_sin, turn_imag, precision=highest
    )
    return values.reshape(channels, length)[:, :seq_len] / length


def short_mix(extended, short_taps, tokens):
    running = jnp.zeros((tokens,) + extended.shape[1:], jnp.float32)
    for lag_index in range(SHORT):
        start_row = SHORT - 1 - lag_index
        running = running + short_taps[lag_index] * extended[start_row : start_row + tokens]
    return running


def mix_long(gate_cols, spec_h, gain, seq_len, tables):
    gate_f = gate_cols.astype(jnp.float32)
    u_real, u_imag = forward_dft(gate_f, tables)
    prod_real = spec_h[0] * u_real - spec_h[1] * u_imag
    prod_imag = spec_h[0] * u_imag + spec_h[1] * u_real
    mix_cols = (inverse_dft(prod_real, prod_imag, seq_len, tables) + gain[:, None] * gate_f).astype(
        jnp.bfloat16
    )
    return (mix_cols, (u_real, u_imag))


def grad_long(grad_cols_in, gate_cols, spec_u, spec_h, gain, seq_len, tables):
    grad_f = grad_cols_in.astype(jnp.float32)
    g_real, g_imag = forward_dft(grad_f, tables)
    back_real = spec_h[0] * g_real + spec_h[1] * g_imag
    back_imag = spec_h[0] * g_imag - spec_h[1] * g_real
    grad_cols = (
        inverse_dft(back_real, back_imag, seq_len, tables) + gain[:, None] * grad_f
    ).astype(jnp.bfloat16)
    corr_real = g_real * spec_u[0] + g_imag * spec_u[1]
    corr_imag = g_imag * spec_u[0] - g_real * spec_u[1]
    grad_filter = inverse_dft(corr_real, corr_imag, seq_len, tables)
    skip_sum = jnp.sum(grad_f * gate_cols.astype(jnp.float32), axis=1)
    return (grad_cols, grad_filter, skip_sum)


def body_factored(projections, short_taps, residues, decay_rates, skip_gain, grad_mixed, out_weight):
    tokens = projections.shape[0]
    seq_len = tokens * lax.axis_size("ctx")
    norm_factor = math.sqrt(seq_len)
    tables = spectral_tables(2 * seq_len)
    earlier = from_behind(projections[tokens - SHORT + 1 :], "ctx", 1)
    ext_proj = jnp.concatenate([earlier, projections], axis=0)
    mixed_in = short_mix(ext_proj, short_taps, tokens)
    query_rows = mixed_in[:, 0]
    key_rows = mixed_in[:, 1]
    value_rows = mixed_in[:, 2]
    gated_rows = (key_rows * value_rows).astype(jnp.bfloat16)
    long_filter, filter_vjp = jax.vjp(partial(make_filter, seq_len=seq_len), residues, decay_rates)
    spec_h = forward_dft(long_filter, tables)
    out_rows = lax.all_gather(grad_mixed, "ch", axis=1, tiled=True)
    grad_out = lax.dot_general(
        out_rows,
        lax.all_gather(out_weight, "ctx", axis=1, tiled=True),
        (((1,), (1,)), ((), ())),
        preferred_element_type=jnp.float32,
    )
    grad_y = (grad_out * query_rows).astype(jnp.bfloat16)
    gate_cols, grad_cols_in = (
        lax.all_to_all(gated_rows.T, "ctx", split_axis=0, concat_axis=1, tiled=True),
        lax.all_to_all(grad_y.T, "ctx", split_axis=0, concat_axis=1, tiled=True),
    )
    mix_cols, spec_u = mix_long(gate_cols, spec_h, skip_gain, seq_len, tables)
    grad_cols, grad_filter, skip_sum = grad_long(
        grad_cols_in, gate_cols, spec_u, spec_h, skip_gain, seq_len, tables
    )
    returned = (
        lax.all_to_all(mix_cols, "ctx", split_axis=1, concat_axis=0, tiled=True),
        lax.all_to_all(grad_cols, "ctx", split_axis=1, concat_axis=0, tiled=True),
    )
    mix_rows = returned[0].T
    grad_gated = returned[1].T
    grad_res, grad_rate = filter_vjp(grad_filter)
    grad_residues = grad_res / norm_factor
    grad_log_rates = grad_rate * decay_rates / norm_factor
    grad_skip = skip_sum / norm_factor
    mixed_out = (query_rows * mix_rows).astype(jnp.bfloat16)
    grad_mix = jnp.stack(
        [grad_out * mix_rows, grad_gated * value_rows, grad_gated * key_rows], axis=1
    )
    later = from_behind(grad_mix[: SHORT - 1], "ctx", -1)
    ext_grad = jnp.concatenate([grad_mix, later], axis=0)
    running = jnp.zeros(grad_mix.shape, jnp.float32)
    short_terms = []
    for lag_index in range(SHORT):
        running = running + short_taps[lag_index] * ext_grad[lag_index : lag_index + tokens]
        start_row = SHORT - 1 - lag_index
        short_terms.append(jnp.sum(grad_mix * ext_proj[start_row : start_row + tokens], axis=0))
    grad_projections = running.astype(jnp.bfloat16)
    grad_short = lax.psum(jnp.stack(short_terms, axis=0), "ctx") / norm_factor
    partial_term = lax.dot_general(
        mixed_out, out_rows, (((0,), (0,)), ((), ())), preferred_element_type=jnp.float32
    )
    weight_sum = lax.psum_scatter(partial_term, "ctx", scatter_dimension=1, tiled=True)
    grad_weight = weight_sum / norm_factor
    return (grad_projections, grad_short, grad_skip, grad_residues, grad_log_rates, grad_weight)


MESH = pl.DeviceIdType.MESH
FINE = 16
ROWS = 64
PAD = 8


def wave_tables(seq_len):
    odd = np.arange(seq_len, dtype=np.int64)[None, :] * 2 + 1
    steps = np.arange(seq_len, dtype=np.int64)[None, :]
    coarse = np.arange(seq_len // FINE, dtype=np.int64)[:, None] * FINE
    fine = np.arange(FINE, dtype=np.int64)[:, None]
    rows = []
    for product in (2 * coarse * steps, (2 * fine + 1) * steps, coarse * odd, fine * odd):
        angle = (product % (4 * seq_len)) * (2.0 * math.pi / (4 * seq_len))
        rows += [np.cos(angle), np.sin(angle)]
    return np.concatenate(rows, axis=0).astype(np.float32)


def dot(a, b):
    return lax.dot_general(a, b, (((1,), (0,)), ((), ())), preferred_element_type=jnp.float32)


def mega(
    proj, w, gm, taps, gain, res, rate, tab,
    o_proj, o_short, o_skip, o_res, o_rate, o_weight,
    pbuf, wbuf, gbuf, mbuf, gp, short_own,
    wh, wl, th, tl, pq, ab, de, sp_h, sp_l, x_h, x_l,
    pf, qkv, gated, gmix, gout, mix, filt, gy, gf,
    loc, s_p, r_p, s_g, r_g, s_gf, r_gf, s_w, r_w, s_wf, r_wf, s_m, r_m, s_o, r_o, s_s, r_s,
):
    f32, bf16 = jnp.float32, jnp.bfloat16
    peers = lax.axis_size("ctx")
    tokens, cols = proj.shape[1], proj.shape[2] // peers
    seq = tokens * peers
    wide = gm.shape[1]
    half = cols // 2
    z = lax.axis_index("ctx")
    k = lax.axis_index("ch")
    g = lax.axis_index("groups")
    norm = math.sqrt(seq)
    hops = range(1, peers)

    def ring(i, d):
        return lax.rem(i + d + peers, peers)

    def span(i, n):
        return pl.ds(pl.multiple_of(i * n, n), n)

    barrier = pltpu.get_barrier_semaphore()
    for d in hops:
        pl.semaphore_signal(barrier, inc=1, device_id={"ctx": ring(z, d)}, device_id_type=MESH)
        pl.semaphore_signal(barrier, inc=1, device_id={"ch": ring(k, d)}, device_id_type=MESH)
    pl.semaphore_signal(barrier, inc=1, device_id={"groups": 1 - g}, device_id_type=MESH)

    def remote(src, dst, ssem, rsem, **where):
        return pltpu.make_async_remote_copy(
            src_ref=src, dst_ref=dst, send_sem=ssem, recv_sem=rsem,
            device_id=where, device_id_type=MESH,
        )

    local = [
        pltpu.make_async_copy(proj.at[:, :, span(z, cols)], pbuf.at[:, span(z, tokens), :], loc.at[0]),
        pltpu.make_async_copy(gm, gbuf.at[k, span(z, tokens), :], loc.at[1]),
        pltpu.make_async_copy(w.at[span(z, cols), :], wbuf.at[z], loc.at[2]),
    ]
    for c in local:
        c.start()
    pl.semaphore_wait(barrier, 2 * (peers - 1) + 1)

    order = (2, 1, 3) if peers == 4 else tuple(hops)
    c_p, c_g, c_w, c_gf, c_wf = {}, {}, {}, {}, {}
    for d in order:
        zp = ring(z, d)
        c_p[d] = remote(proj.at[:, :, span(zp, cols)], pbuf.at[:, span(z, tokens), :], s_p.at[d - 1], r_p.at[d - 1], ctx=zp)
        c_p[d].start()
    for d in order:
        zp = ring(z, d)
        c_g[d] = remote(gm, gbuf.at[k, span(z, tokens), :], s_g.at[d - 1], r_g.at[d - 1], ctx=zp)
        c_g[d].start()
    for d in order:
        zp = ring(z, d)
        c_w[d] = remote(
            w.at[pl.ds(pl.multiple_of(zp * cols + g * half, half), half), :],
            wbuf.at[z, span(g, half), :], s_w.at[d - 1], r_w.at[d - 1], ctx=zp,
        )
        c_w[d].start()
    for e in hops:
        c_gf[0, e] = remote(gm, gbuf.at[k, span(z, tokens), :], s_gf.at[e - 1], r_gf.at[e - 1], ch=ring(k, e))
        c_gf[0, e].start()

    groups_of = seq // FINE
    at = [0]
    for n in (groups_of, groups_of, FINE, FINE, groups_of, groups_of, FINE, FINE):
        at.append(at[-1] + n)

    def put(high, low, rows, columns, x):
        top = x.astype(bf16)
        high[rows, columns] = top
        low[rows, columns] = (x - top.astype(f32)).astype(bf16)

    def fill(i, carry):
        for base, high, low, by_row in ((0, wh, wl, True), (4, th, tl, False)):
            ca, sa = tab[pl.ds(at[base] + i, 1), :], tab[pl.ds(at[base + 1] + i, 1), :]
            cb, sb = tab[at[base + 2] : at[base + 3], :], tab[at[base + 3] : at[base + 4], :]
            cos, sin = ca * cb - sa * sb, sa * cb + ca * sb
            first = pl.multiple_of(i * FINE, FINE)
            if by_row:
                put(high, low, pl.ds(first, FINE), slice(None), cos)
                put(high, low, pl.ds(pl.multiple_of(seq + i * FINE, FINE), FINE), slice(None), sin)
            else:
                put(high, low, pl.ds(first, FINE), slice(0, seq), cos)
                put(high, low, pl.ds(first, FINE), slice(seq, 2 * seq), sin)
        return carry

    lax.fori_loop(0, groups_of, fill, 0)

    order_n = res.shape[0]
    amp = jnp.sqrt(2.0 * rate[...] / seq)
    scaled = res[...] * amp
    for r in range(0, seq, ROWS):
        where = (lax.broadcasted_iota(jnp.int32, (ROWS, cols), 0) + r).astype(f32) / seq
        total = jnp.zeros((ROWS, cols), f32)
        for n in range(order_n):
            total = total + scaled[n : n + 1] * jnp.exp(-rate[n : n + 1, :] * where)
        put(x_h, x_l, slice(r, r + ROWS), slice(None), total)
    block = 256
    for r in range(0, 2 * seq, block):
        rows = slice(r, r + block)
        pq[rows] = dot(wh[rows], x_h[...]) + dot(wl[rows], x_h[...]) + dot(wh[rows], x_l[...])

    def spectrum(out, x):
        for r in range(0, 2 * seq, block):
            rows = slice(r, r + block)
            out[rows] = dot(wh[rows], x[...]) + dot(wl[rows], x[...])

    def product(x, y, conj):
        for r in range(0, seq, ROWS):
            lo, hi = slice(r, r + ROWS), slice(seq + r, seq + r + ROWS)
            a, b, c, d = x[lo], x[hi], y[lo], y[hi]
            if conj:
                put(sp_h, sp_l, lo, slice(None), a * c + b * d)
                put(sp_h, sp_l, hi, slice(None), a * d - b * c)
            else:
                put(sp_h, sp_l, lo, slice(None), a * c - b * d)
                put(sp_h, sp_l, hi, slice(None), a * d + b * c)

    def inverse(r, n):
        rows = slice(r, r + n)
        total = dot(th[rows], sp_h[...]) + dot(tl[rows], sp_h[...]) + dot(th[rows], sp_l[...])
        return total * (1.0 / seq)

    for i in range(3):
        pf[i, 0:PAD] = jnp.zeros((PAD, cols), f32)
        gmix[i, seq : seq + PAD] = jnp.zeros((PAD, cols), f32)
    gain_row = gain[...]

    local[0].wait()
    for d in order:
        c_p[d].wait_recv()
    for r in range(0, seq, ROWS):
        for i in range(3):
            pf[i, PAD + r : PAD + r + ROWS] = pbuf[i, r : r + ROWS].astype(f32)
        for i in range(3):
            total = jnp.zeros((ROWS, cols), f32)
            for j in range(SHORT):
                total = total + taps[3 * j + i : 3 * j + i + 1] * pf[i, PAD + r - j : PAD + r - j + ROWS]
            qkv[i, r : r + ROWS] = total
        gated[r : r + ROWS] = (qkv[1, r : r + ROWS] * qkv[2, r : r + ROWS]).astype(bf16)
    spectrum(ab, gated)
    product(pq, ab, False)
    for r in range(0, seq, block):
        rows = slice(r, r + block)
        m = (inverse(r, block) + gain_row * gated[rows].astype(f32)).astype(bf16).astype(f32)
        mix[rows] = m
        mbuf[z, :, rows] = (qkv[0, rows] * m).T.astype(bf16)

    local[1].wait()
    local[2].wait()
    for d in order:
        c_g[d].wait_recv()
        zs = ring(z, -d)
        for e in hops:
            part = gbuf.at[k, span(zs, tokens), :]
            i = d * (peers - 1) + e - 1
            c_gf[d, e] = remote(part, part, s_gf.at[i], r_gf.at[i], ch=ring(k, e))
            c_gf[d, e].start()
    for d in order:
        c_w[d].wait_recv()
        part = wbuf.at[ring(z, -d), span(g, half), :]
        c_wf[d] = remote(part, part, s_wf.at[d - 1], r_wf.at[d - 1], groups=1 - g)
        c_wf[d].start()
    c_m = {}
    for d in order:
        c_m[d] = remote(mbuf.at[z], mbuf.at[z], s_m.at[d - 1], r_m.at[d - 1], ctx=ring(z, d))
        c_m[d].start()
    for key in c_gf:
        c_gf[key].wait_recv()
    for d in order:
        c_wf[d].wait_recv()

    for r in range(0, seq, block):
        rows = slice(r, r + block)
        total = jnp.zeros((block, cols), f32)
        for j in range(peers):
            total = total + lax.dot_general(
                gbuf[j, rows, :], wbuf[j], (((1,), (1,)), ((), ())), preferred_element_type=f32
            )
        gout[rows] = total
    for r in range(0, seq, ROWS):
        rows = slice(r, r + ROWS)
        go = gout[rows]
        gy[rows] = (go * qkv[0, rows]).astype(bf16)
        gmix[0, rows] = go * mix[rows]
    spectrum(de, gy)
    product(pq, de, True)
    for r in range(0, seq, block):
        rows = slice(r, r + block)
        gg = (inverse(r, block) + gain_row * gy[rows].astype(f32)).astype(bf16).astype(f32)
        gmix[1, rows] = gg * qkv[2, rows]
        gmix[2, rows] = gg * qkv[1, rows]
    for r in range(0, seq, ROWS):
        for i in range(3):
            total = jnp.zeros((ROWS, cols), f32)
            for j in range(SHORT):
                total = total + taps[3 * j + i : 3 * j + i + 1] * gmix[i, r + j : r + j + ROWS]
            gp[i, r : r + ROWS] = total.astype(bf16)
    c_o, c_s = {}, {}
    for d in order:
        zp = ring(z, d)
        c_o[d] = remote(gp.at[:, span(zp, tokens), :], o_proj.at[:, :, span(z, cols)], s_o.at[d - 1], r_o.at[d - 1], ctx=zp)
        c_o[d].start()
    own = pltpu.make_async_copy(gp.at[:, span(z, tokens), :], o_proj.at[:, :, span(z, cols)], loc.at[3])
    own.start()

    def fold(x):
        return jnp.sum(x.reshape(ROWS // 8, 8, cols), axis=0)

    for i in range(3):
        sums = [jnp.zeros((8, cols), f32) for _ in range(SHORT)]
        for r in range(0, seq, ROWS):
            here = gmix[i, r : r + ROWS]
            for j in range(SHORT):
                sums[j] = sums[j] + fold(here * pf[i, PAD + r - j : PAD + r - j + ROWS])
        for j in range(SHORT):
            short_own[3 * j + i : 3 * j + i + 1, :] = jnp.sum(sums[j], axis=0, keepdims=True) / norm
    for j in range(9, 16):
        short_own[j : j + 1, :] = jnp.zeros((1, cols), f32)
    for d in order:
        c_s[d] = remote(short_own, o_short.at[:, span(z, cols)], s_s.at[d - 1], r_s.at[d - 1], ctx=ring(z, d))
        c_s[d].start()
    own_short = pltpu.make_async_copy(short_own, o_short.at[:, span(z, cols)], loc.at[4])
    own_short.start()
    skip = jnp.zeros((8, cols), f32)
    for r in range(0, seq, ROWS):
        rows = slice(r, r + ROWS)
        skip = skip + fold(gy[rows].astype(f32) * gated[rows].astype(f32))
    o_skip[...] = jnp.sum(skip, axis=0, keepdims=True) / norm
    product(ab, de, True)
    for r in range(0, seq, block):
        gf[r : r + block] = inverse(r, block)

    def moments(n, carry):
        decay = rate[pl.ds(n, 1), :]
        sum0 = jnp.zeros((8, cols), f32)
        sum1 = jnp.zeros((8, cols), f32)
        for r in range(0, seq, ROWS):
            where = (lax.broadcasted_iota(jnp.int32, (ROWS, cols), 0) + r).astype(f32) / seq
            term = jnp.exp(-decay * where) * gf[r : r + ROWS]
            sum0 = sum0 + fold(term)
            sum1 = sum1 + fold(term * where)
        m0 = jnp.sum(sum0, axis=0, keepdims=True)
        m1 = jnp.sum(sum1, axis=0, keepdims=True)
        size = jnp.sqrt(2.0 * decay / seq)
        o_res[pl.ds(n, 1), :] = size * m0 / norm
        o_rate[pl.ds(n, 1), :] = res[pl.ds(n, 1), :] * size * (0.5 * m0 - decay * m1) / norm
        return carry

    lax.fori_loop(0, order_n, moments, 0)

    def weight(zs):
        o_weight[span(zs, cols), :] = dot(mbuf[zs], gbuf[z]) * (1.0 / norm)

    weight(z)
    for d in (1, 3, 2) if peers == 4 else hops:
        c_m[d].wait_recv()
        weight(ring(z, -d))
    for group in (c_o, c_s):
        for d in order:
            group[d].wait_recv()
    own.wait()
    own_short.wait()
    for group in (c_p, c_g, c_w, c_gf, c_wf, c_m, c_o, c_s):
        for key in group:
            group[key].wait_send()


def body(projections, short_taps, residues, decay_rates, skip_gain, grad_mixed, out_weight):
    tokens, _, width = projections.shape
    peers = lax.axis_size("ctx")
    seq = tokens * peers
    if seq > 1024 or lax.axis_size("ch") != peers or lax.axis_size("groups") != 2:
        return body_factored(
            projections, short_taps, residues, decay_rates, skip_gain, grad_mixed, out_weight
        )
    cols = width // peers
    wide = grad_mixed.shape[1]
    f32, bf16 = jnp.float32, jnp.bfloat16
    taps = lax.dynamic_slice_in_dim(short_taps, lax.axis_index("ctx") * cols, cols, 2)
    taps = taps.reshape(SHORT * 3, cols)
    tables = jnp.asarray(wave_tables(seq))
    order = residues.shape[1]
    vmem = pl.BlockSpec(memory_space=pltpu.VMEM)
    any_ = pl.BlockSpec(memory_space=pl.ANY)
    near = peers - 1
    dma = pltpu.SemaphoreType.DMA
    S = jax.ShapeDtypeStruct
    V = pltpu.VMEM
    outs = pl.pallas_call(
        mega,
        out_shape=(
            S((3, tokens, width), bf16), S((16, width), f32), S((1, cols), f32),
            S((order, cols), f32), S((order, cols), f32), S((width, wide), f32),
        ),
        in_specs=[any_, any_, any_] + [vmem] * 5,
        out_specs=[vmem] * 6,
        scratch_shapes=[
            V((3, seq, cols), bf16), V((peers, cols, wide), bf16), V((peers, seq, wide), bf16),
            V((peers, cols, seq), bf16), V((3, seq, cols), bf16), V((16, cols), f32),
            V((2 * seq, seq), bf16), V((2 * seq, seq), bf16), V((seq, 2 * seq), bf16), V((seq, 2 * seq), bf16),
            V((2 * seq, cols), f32), V((2 * seq, cols), f32), V((2 * seq, cols), f32),
            V((2 * seq, cols), bf16), V((2 * seq, cols), bf16), V((seq, cols), bf16), V((seq, cols), bf16),
            V((3, PAD + seq, cols), f32), V((3, seq, cols), f32), V((seq, cols), bf16),
            V((3, seq + PAD, cols), f32), V((seq, cols), f32), V((seq, cols), f32), V((8, cols), f32),
            V((seq, cols), bf16), V((seq, cols), f32),
            dma((5,)), dma((near,)), dma((near,)), dma((near,)), dma((near,)),
            dma((peers * near,)), dma((peers * near,)), dma((near,)), dma((near,)), dma((near,)), dma((near,)),
            dma((near,)), dma((near,)), dma((near,)), dma((near,)), dma((near,)), dma((near,)),
        ],
        compiler_params=pltpu.CompilerParams(
            collective_id=0, has_side_effects=True, vmem_limit_bytes=56 * 1024 * 1024
        ),
    )(
        projections.transpose(1, 0, 2), out_weight, grad_mixed, taps, skip_gain[None],
        residues.T, decay_rates.T, tables,
    )
    grad_proj, short, skip, grad_res, grad_rate, grad_weight = outs
    return (
        grad_proj.transpose(1, 0, 2),
        short[: SHORT * 3].reshape(SHORT, 3, width),
        skip[0],
        grad_res.T,
        grad_rate.T,
        grad_weight,
    )


def solution(mesh):
    return jax.shard_map(
        body,
        mesh=mesh,
        in_specs=(
            P(("groups", "ctx"), None, "ch"),
            P(None, None, "ch"),
            P(("ch", "ctx"), None),
            P(("ch", "ctx"), None),
            P(("ch", "ctx")),
            P(("groups", "ctx"), "ch"),
            P("ch", "ctx"),
        ),
        out_specs=(
            P(("groups", "ctx"), None, "ch"),
            P("groups", None, "ch"),
            P(("groups", "ch", "ctx")),
            P(("groups", "ch", "ctx"), None),
            P(("groups", "ch", "ctx"), None),
            P(("groups", "ch"), "ctx"),
        ),
        check_vma=False,
    )
```

```python
from functools import partial
import math

import jax
import jax.numpy as jnp
import numpy as np
from jax import lax
from jax.experimental import pallas as pl
from jax.experimental.pallas import tpu as pltpu
from jax.sharding import PartitionSpec as P

SHORT = 3


def from_behind(x, axis, by):
    peers = lax.axis_size(axis)
    pairs = [(i, i + by) for i in range(peers) if 0 <= i + by < peers]
    return lax.ppermute(x, axis, pairs)


def make_filter(residues, decay_rates, seq_len):
    positions = jnp.arange(seq_len, dtype=jnp.float32) / seq_len
    amplitude = residues * jnp.sqrt(2.0 * decay_rates / seq_len)
    basis = jnp.exp(-decay_rates[:, :, None] * positions[None, None, :])
    return jnp.einsum("cn,cnt->ct", amplitude, basis, precision=lax.Precision.HIGHEST)


def circle(rows_count, cols_count, period):
    left_idx = jnp.arange(rows_count, dtype=jnp.int32)[:, None]
    right_idx = jnp.arange(cols_count, dtype=jnp.int32)[None, :]
    angle = (left_idx * right_idx % period).astype(jnp.float32) * (2.0 * math.pi / period)
    return (jnp.cos(angle), jnp.sin(angle))


def spectral_tables(length):
    factor_a = 1
    while factor_a * factor_a * 4 <= length and length % (factor_a * 2) == 0:
        factor_a = factor_a * 2
    factor_b = length // factor_a
    a_cos, a_sin = circle(factor_a, factor_a, factor_a)
    b_cos, b_sin = circle(factor_b, factor_b, factor_b)
    t_cos, t_sin = circle(factor_a, factor_b, length)
    return (length, factor_a, factor_b, a_cos, a_sin, b_cos, b_sin, t_cos, t_sin)


def forward_dft(signal, tables):
    length, factor_a, factor_b, a_cos, a_sin, b_cos, b_sin, t_cos, t_sin = tables
    highest = lax.Precision.HIGHEST
    channels, seq_len = signal.shape
    grid = jnp.pad(signal, ((0, 0), (0, length - seq_len))).reshape(channels, factor_a, factor_b)
    part_real = jnp.einsum("ka,cab->ckb", a_cos, grid, precision=highest)
    part_imag = -jnp.einsum("ka,cab->ckb", a_sin, grid, precision=highest)
    turn_real = part_real * t_cos + part_imag * t_sin
    turn_imag = part_imag * t_cos - part_real * t_sin
    out_real = jnp.einsum("ckb,bm->ckm", turn_real, b_cos, precision=highest) + jnp.einsum(
        "ckb,bm->ckm", turn_imag, b_sin, precision=highest
    )
    out_imag = jnp.einsum("ckb,bm->ckm", turn_imag, b_cos, precision=highest) - jnp.einsum(
        "ckb,bm->ckm", turn_real, b_sin, precision=highest
    )
    return (out_real, out_imag)


def inverse_dft(spec_real, spec_imag, seq_len, tables):
    length, factor_a, factor_b, a_cos, a_sin, b_cos, b_sin, t_cos, t_sin = tables
    highest = lax.Precision.HIGHEST
    channels = spec_real.shape[0]
    mid_real = jnp.einsum("ckm,mb->ckb", spec_real, b_cos, precision=highest) - jnp.einsum(
        "ckm,mb->ckb", spec_imag, b_sin, precision=highest
    )
    mid_imag = jnp.einsum("ckm,mb->ckb", spec_imag, b_cos, precision=highest) + jnp.einsum(
        "ckm,mb->ckb", spec_real, b_sin, precision=highest
    )
    turn_real = mid_real * t_cos - mid_imag * t_sin
    turn_imag = mid_imag * t_cos + mid_real * t_sin
    values = jnp.einsum("ak,ckb->cab", a_cos, turn_real, precision=highest) - jnp.einsum(
        "ak,ckb->cab", a_sin, turn_imag, precision=highest
    )
    return values.reshape(channels, length)[:, :seq_len] / length


def short_mix(extended, short_taps, tokens):
    running = jnp.zeros((tokens,) + extended.shape[1:], jnp.float32)
    for lag_index in range(SHORT):
        start_row = SHORT - 1 - lag_index
        running = running + short_taps[lag_index] * extended[start_row : start_row + tokens]
    return running


def mix_long(gate_cols, spec_h, gain, seq_len, tables):
    gate_f = gate_cols.astype(jnp.float32)
    u_real, u_imag = forward_dft(gate_f, tables)
    prod_real = spec_h[0] * u_real - spec_h[1] * u_imag
    prod_imag = spec_h[0] * u_imag + spec_h[1] * u_real
    mix_cols = (inverse_dft(prod_real, prod_imag, seq_len, tables) + gain[:, None] * gate_f).astype(
        jnp.bfloat16
    )
    return (mix_cols, (u_real, u_imag))


def grad_long(grad_cols_in, gate_cols, spec_u, spec_h, gain, seq_len, tables):
    grad_f = grad_cols_in.astype(jnp.float32)
    g_real, g_imag = forward_dft(grad_f, tables)
    back_real = spec_h[0] * g_real + spec_h[1] * g_imag
    back_imag = spec_h[0] * g_imag - spec_h[1] * g_real
    grad_cols = (
        inverse_dft(back_real, back_imag, seq_len, tables) + gain[:, None] * grad_f
    ).astype(jnp.bfloat16)
    corr_real = g_real * spec_u[0] + g_imag * spec_u[1]
    corr_imag = g_imag * spec_u[0] - g_real * spec_u[1]
    grad_filter = inverse_dft(corr_real, corr_imag, seq_len, tables)
    skip_sum = jnp.sum(grad_f * gate_cols.astype(jnp.float32), axis=1)
    return (grad_cols, grad_filter, skip_sum)


def body_factored(projections, short_taps, residues, decay_rates, skip_gain, grad_mixed, out_weight):
    tokens = projections.shape[0]
    seq_len = tokens * lax.axis_size("ctx")
    norm_factor = math.sqrt(seq_len)
    tables = spectral_tables(2 * seq_len)
    earlier = from_behind(projections[tokens - SHORT + 1 :], "ctx", 1)
    ext_proj = jnp.concatenate([earlier, projections], axis=0)
    mixed_in = short_mix(ext_proj, short_taps, tokens)
    query_rows = mixed_in[:, 0]
    key_rows = mixed_in[:, 1]
    value_rows = mixed_in[:, 2]
    gated_rows = (key_rows * value_rows).astype(jnp.bfloat16)
    long_filter, filter_vjp = jax.vjp(partial(make_filter, seq_len=seq_len), residues, decay_rates)
    spec_h = forward_dft(long_filter, tables)
    out_rows = lax.all_gather(grad_mixed, "ch", axis=1, tiled=True)
    grad_out = lax.dot_general(
        out_rows,
        lax.all_gather(out_weight, "ctx", axis=1, tiled=True),
        (((1,), (1,)), ((), ())),
        preferred_element_type=jnp.float32,
    )
    grad_y = (grad_out * query_rows).astype(jnp.bfloat16)
    gate_cols, grad_cols_in = (
        lax.all_to_all(gated_rows.T, "ctx", split_axis=0, concat_axis=1, tiled=True),
        lax.all_to_all(grad_y.T, "ctx", split_axis=0, concat_axis=1, tiled=True),
    )
    mix_cols, spec_u = mix_long(gate_cols, spec_h, skip_gain, seq_len, tables)
    grad_cols, grad_filter, skip_sum = grad_long(
        grad_cols_in, gate_cols, spec_u, spec_h, skip_gain, seq_len, tables
    )
    returned = (
        lax.all_to_all(mix_cols, "ctx", split_axis=1, concat_axis=0, tiled=True),
        lax.all_to_all(grad_cols, "ctx", split_axis=1, concat_axis=0, tiled=True),
    )
    mix_rows = returned[0].T
    grad_gated = returned[1].T
    grad_res, grad_rate = filter_vjp(grad_filter)
    grad_residues = grad_res / norm_factor
    grad_log_rates = grad_rate * decay_rates / norm_factor
    grad_skip = skip_sum / norm_factor
    mixed_out = (query_rows * mix_rows).astype(jnp.bfloat16)
    grad_mix = jnp.stack(
        [grad_out * mix_rows, grad_gated * value_rows, grad_gated * key_rows], axis=1
    )
    later = from_behind(grad_mix[: SHORT - 1], "ctx", -1)
    ext_grad = jnp.concatenate([grad_mix, later], axis=0)
    running = jnp.zeros(grad_mix.shape, jnp.float32)
    short_terms = []
    for lag_index in range(SHORT):
        running = running + short_taps[lag_index] * ext_grad[lag_index : lag_index + tokens]
        start_row = SHORT - 1 - lag_index
        short_terms.append(jnp.sum(grad_mix * ext_proj[start_row : start_row + tokens], axis=0))
    grad_projections = running.astype(jnp.bfloat16)
    grad_short = lax.psum(jnp.stack(short_terms, axis=0), "ctx") / norm_factor
    partial_term = lax.dot_general(
        mixed_out, out_rows, (((0,), (0,)), ((), ())), preferred_element_type=jnp.float32
    )
    weight_sum = lax.psum_scatter(partial_term, "ctx", scatter_dimension=1, tiled=True)
    grad_weight = weight_sum / norm_factor
    return (grad_projections, grad_short, grad_skip, grad_residues, grad_log_rates, grad_weight)


MESH = pl.DeviceIdType.MESH
FINE = 16
ROWS = 64
PAD = 8


def wave_tables(seq_len):
    odd = np.arange(seq_len, dtype=np.int64)[None, :] * 2 + 1
    steps = np.arange(seq_len, dtype=np.int64)[None, :]
    coarse = np.arange(seq_len // FINE, dtype=np.int64)[:, None] * FINE
    fine = np.arange(FINE, dtype=np.int64)[:, None]
    rows = []
    for product in (2 * coarse * steps, (2 * fine + 1) * steps, coarse * odd, fine * odd):
        angle = (product % (4 * seq_len)) * (2.0 * math.pi / (4 * seq_len))
        rows += [np.cos(angle), np.sin(angle)]
    return np.concatenate(rows, axis=0).astype(np.float32)


def dot(a, b):
    return lax.dot_general(a, b, (((1,), (0,)), ((), ())), preferred_element_type=jnp.float32)


def mega(
    proj, w, gm, taps, gain, res, rate, tab,
    o_proj, o_short, o_skip, o_res, o_rate, o_weight,
    pbuf, wbuf, gbuf, mbuf, gp, short_own,
    wh, wl, th, tl, pq, ab, de, sp_h, sp_l, x_h, x_l,
    pf, qkv, gated, gmix, gout, mix, filt, gy, gf,
    loc, s_p, r_p, s_g, r_g, s_gf, r_gf, s_w, r_w, s_wf, r_wf, s_m, r_m, s_o, r_o, s_s, r_s,
):
    f32, bf16 = jnp.float32, jnp.bfloat16
    peers = lax.axis_size("ctx")
    tokens, cols = proj.shape[1], proj.shape[2] // peers
    seq = tokens * peers
    wide = gm.shape[1]
    half = cols // 2
    z = lax.axis_index("ctx")
    k = lax.axis_index("ch")
    g = lax.axis_index("groups")
    norm = math.sqrt(seq)
    hops = range(1, peers)

    def ring(i, d):
        return lax.rem(i + d + peers, peers)

    def span(i, n):
        return pl.ds(pl.multiple_of(i * n, n), n)

    barrier = pltpu.get_barrier_semaphore()
    for d in hops:
        pl.semaphore_signal(barrier, inc=1, device_id={"ctx": ring(z, d)}, device_id_type=MESH)
        pl.semaphore_signal(barrier, inc=1, device_id={"ch": ring(k, d)}, device_id_type=MESH)
    pl.semaphore_signal(barrier, inc=1, device_id={"groups": 1 - g}, device_id_type=MESH)

    def remote(src, dst, ssem, rsem, **where):
        return pltpu.make_async_remote_copy(
            src_ref=src, dst_ref=dst, send_sem=ssem, recv_sem=rsem,
            device_id=where, device_id_type=MESH,
        )

    local = [
        pltpu.make_async_copy(proj.at[:, :, span(z, cols)], pbuf.at[:, span(z, tokens), :], loc.at[0]),
        pltpu.make_async_copy(gm, gbuf.at[k, span(z, tokens), :], loc.at[1]),
        pltpu.make_async_copy(w.at[span(z, cols), :], wbuf.at[z], loc.at[2]),
    ]
    for c in local:
        c.start()
    pl.semaphore_wait(barrier, 2 * (peers - 1) + 1)

    order = (2, 1, 3)
    c_p, c_w, c_wf = {}, {}, {}
    mate = k + 1 - 2 * lax.rem(k, 2)
    across = lax.rem(k + 2, 4)

    def line(i, side, block, ssem, rsem):
        slot = block(ring(z, -side * i))
        sem = i if side > 0 else peers - 1 + i
        return remote(slot, slot, ssem.at[sem], rsem.at[sem], ctx=ring(z, side))

    def line_sends(i, side):
        return (z + 1 < peers) & (z >= i) if side > 0 else (z >= 1) & (z + i < peers)

    def line_gets(i, side):
        return z >= i + 1 if side > 0 else z + i + 1 < peers

    def line_start(i, block, ssem, rsem):
        for side in (1, -1):
            @pl.when(line_sends(i, side))
            def _():
                line(i, side, block, ssem, rsem).start()

    def line_step(i, block, ssem, rsem, then=None):
        for side in (1, -1):
            @pl.when(line_gets(i, side))
            def _():
                line(i, side, block, ssem, rsem).wait_recv()
                if then is not None:
                    then(ring(z, -side * (i + 1)))
        if i + 1 < peers - 1:
            line_start(i + 1, block, ssem, rsem)

    def line_end(block, ssem, rsem):
        for i in range(peers - 1):
            for side in (1, -1):
                @pl.when(line_sends(i, side))
                def _():
                    line(i, side, block, ssem, rsem).wait_send()

    def gm_block(zs):
        return gbuf.at[k, span(zs, tokens), :]

    def gm_out(zs, where):
        n = zs + peers * where
        column = (k, k, across)[where]
        part = gbuf.at[column, span(zs, tokens), :]
        return remote(part, part, s_gf.at[n], r_gf.at[n], ch=(mate, across, mate)[where])

    def gm_spread(zs):
        gm_out(zs, 1).start()
        gm_out(zs, 0).start()

    def mixed_block(zs):
        return mbuf.at[zs]

    local[1].wait()
    line_start(0, gm_block, s_g, r_g)
    gm_spread(z)
    for d in order:
        zp = ring(z, d)
        c_p[d] = remote(proj.at[:, :, span(zp, cols)], pbuf.at[:, span(z, tokens), :], s_p.at[d - 1], r_p.at[d - 1], ctx=zp)
        c_p[d].start()
    for d in order:
        zp = ring(z, d)
        c_w[d] = remote(
            w.at[pl.ds(pl.multiple_of(zp * cols + g * half, half), half), :],
            wbuf.at[z, span(g, half), :], s_w.at[d - 1], r_w.at[d - 1], ctx=zp,
        )
        c_w[d].start()
    groups_of = seq // FINE
    at = [0]
    for n in (groups_of, groups_of, FINE, FINE, groups_of, groups_of, FINE, FINE):
        at.append(at[-1] + n)

    def put(high, low, rows, columns, x):
        top = x.astype(bf16)
        high[rows, columns] = top
        low[rows, columns] = (x - top.astype(f32)).astype(bf16)

    def fill(i, carry):
        for base, high, low, by_row in ((0, wh, wl, True), (4, th, tl, False)):
            ca, sa = tab[pl.ds(at[base] + i, 1), :], tab[pl.ds(at[base + 1] + i, 1), :]
            cb, sb = tab[at[base + 2] : at[base + 3], :], tab[at[base + 3] : at[base + 4], :]
            cos, sin = ca * cb - sa * sb, sa * cb + ca * sb
            first = pl.multiple_of(i * FINE, FINE)
            if by_row:
                put(high, low, pl.ds(first, FINE), slice(None), cos)
                put(high, low, pl.ds(pl.multiple_of(seq + i * FINE, FINE), FINE), slice(None), sin)
            else:
                put(high, low, pl.ds(first, FINE), slice(0, seq), cos)
                put(high, low, pl.ds(first, FINE), slice(seq, 2 * seq), sin)
        return carry

    lax.fori_loop(0, groups_of, fill, 0)
    line_step(0, gm_block, s_g, r_g, gm_spread)

    order_n = res.shape[0]
    amp = jnp.sqrt(2.0 * rate[...] / seq)
    scaled = res[...] * amp
    for r in range(0, seq, ROWS):
        where = (lax.broadcasted_iota(jnp.int32, (ROWS, cols), 0) + r).astype(f32) / seq
        total = jnp.zeros((ROWS, cols), f32)
        for n in range(order_n):
            total = total + scaled[n : n + 1] * jnp.exp(-rate[n : n + 1, :] * where)
        put(x_h, x_l, slice(r, r + ROWS), slice(None), total)
    line_step(1, gm_block, s_g, r_g, gm_spread)
    block = 256
    for r in range(0, 2 * seq, block):
        rows = slice(r, r + block)
        pq[rows] = dot(wh[rows], x_h[...]) + dot(wl[rows], x_h[...]) + dot(wh[rows], x_l[...])

    line_step(2, gm_block, s_g, r_g, gm_spread)

    def spectrum(out, x):
        for r in range(0, 2 * seq, block):
            rows = slice(r, r + block)
            out[rows] = dot(wh[rows], x[...]) + dot(wl[rows], x[...])

    def product(x, y, conj):
        for r in range(0, seq, ROWS):
            lo, hi = slice(r, r + ROWS), slice(seq + r, seq + r + ROWS)
            a, b, c, d = x[lo], x[hi], y[lo], y[hi]
            if conj:
                put(sp_h, sp_l, lo, slice(None), a * c + b * d)
                put(sp_h, sp_l, hi, slice(None), a * d - b * c)
            else:
                put(sp_h, sp_l, lo, slice(None), a * c - b * d)
                put(sp_h, sp_l, hi, slice(None), a * d + b * c)

    def inverse(r, n):
        rows = slice(r, r + n)
        total = dot(th[rows], sp_h[...]) + dot(tl[rows], sp_h[...]) + dot(th[rows], sp_l[...])
        return total * (1.0 / seq)

    for i in range(3):
        pf[i, 0:PAD] = jnp.zeros((PAD, cols), f32)
        gmix[i, seq : seq + PAD] = jnp.zeros((PAD, cols), f32)
    gain_row = gain[...]

    local[0].wait()
    for d in order:
        c_p[d].wait_recv()
    for r in range(0, seq, ROWS):
        for i in range(3):
            pf[i, PAD + r : PAD + r + ROWS] = pbuf[i, r : r + ROWS].astype(f32)
        for i in range(3):
            total = jnp.zeros((ROWS, cols), f32)
            for j in range(SHORT):
                total = total + taps[3 * j + i : 3 * j + i + 1] * pf[i, PAD + r - j : PAD + r - j + ROWS]
            qkv[i, r : r + ROWS] = total
        gated[r : r + ROWS] = (qkv[1, r : r + ROWS] * qkv[2, r : r + ROWS]).astype(bf16)
    spectrum(ab, gated)
    product(pq, ab, False)
    for r in range(0, seq, block):
        rows = slice(r, r + block)
        m = (inverse(r, block) + gain_row * gated[rows].astype(f32)).astype(bf16).astype(f32)
        mix[rows] = m
        mbuf[z, :, rows] = (qkv[0, rows] * m).T.astype(bf16)

    line_start(0, mixed_block, s_m, r_m)
    local[2].wait()
    for zs in range(peers):
        gm_out(zs, 1).wait_recv()
        gm_out(zs, 2).start()
    for d in order:
        c_w[d].wait_recv()
        part = wbuf.at[ring(z, -d), span(g, half), :]
        c_wf[d] = remote(part, part, s_wf.at[d - 1], r_wf.at[d - 1], groups=1 - g)
        c_wf[d].start()
    line_step(0, mixed_block, s_m, r_m)
    for zs in range(peers):
        gm_out(zs, 0).wait_recv()
        gm_out(zs, 2).wait_recv()
    for d in order:
        c_wf[d].wait_recv()

    for r in range(0, seq, block):
        rows = slice(r, r + block)
        total = jnp.zeros((block, cols), f32)
        for j in range(peers):
            total = total + lax.dot_general(
                gbuf[j, rows, :], wbuf[j], (((1,), (1,)), ((), ())), preferred_element_type=f32
            )
        gout[rows] = total
    for r in range(0, seq, ROWS):
        rows = slice(r, r + ROWS)
        go = gout[rows]
        gy[rows] = (go * qkv[0, rows]).astype(bf16)
        gmix[0, rows] = go * mix[rows]
    spectrum(de, gy)
    product(pq, de, True)
    line_step(1, mixed_block, s_m, r_m)
    for r in range(0, seq, block):
        rows = slice(r, r + block)
        gg = (inverse(r, block) + gain_row * gy[rows].astype(f32)).astype(bf16).astype(f32)
        gmix[1, rows] = gg * qkv[2, rows]
        gmix[2, rows] = gg * qkv[1, rows]
    for r in range(0, seq, ROWS):
        for i in range(3):
            total = jnp.zeros((ROWS, cols), f32)
            for j in range(SHORT):
                total = total + taps[3 * j + i : 3 * j + i + 1] * gmix[i, r + j : r + j + ROWS]
            gp[i, r : r + ROWS] = total.astype(bf16)
    c_o, c_s = {}, {}
    for d in order:
        zp = ring(z, d)
        c_o[d] = remote(gp.at[:, span(zp, tokens), :], o_proj.at[:, :, span(z, cols)], s_o.at[d - 1], r_o.at[d - 1], ctx=zp)
        c_o[d].start()
    own = pltpu.make_async_copy(gp.at[:, span(z, tokens), :], o_proj.at[:, :, span(z, cols)], loc.at[3])
    own.start()

    def fold(x):
        return jnp.sum(x.reshape(ROWS // 8, 8, cols), axis=0)

    for i in range(3):
        sums = [jnp.zeros((8, cols), f32) for _ in range(SHORT)]
        for r in range(0, seq, ROWS):
            here = gmix[i, r : r + ROWS]
            for j in range(SHORT):
                sums[j] = sums[j] + fold(here * pf[i, PAD + r - j : PAD + r - j + ROWS])
        for j in range(SHORT):
            short_own[3 * j + i : 3 * j + i + 1, :] = jnp.sum(sums[j], axis=0, keepdims=True) / norm
    for j in range(9, 16):
        short_own[j : j + 1, :] = jnp.zeros((1, cols), f32)
    for d in order:
        c_s[d] = remote(short_own, o_short.at[:, span(z, cols)], s_s.at[d - 1], r_s.at[d - 1], ctx=ring(z, d))
        c_s[d].start()
    own_short = pltpu.make_async_copy(short_own, o_short.at[:, span(z, cols)], loc.at[4])
    own_short.start()
    skip = jnp.zeros((8, cols), f32)
    for r in range(0, seq, ROWS):
        rows = slice(r, r + ROWS)
        skip = skip + fold(gy[rows].astype(f32) * gated[rows].astype(f32))
    o_skip[...] = jnp.sum(skip, axis=0, keepdims=True) / norm
    product(ab, de, True)
    for r in range(0, seq, block):
        gf[r : r + block] = inverse(r, block)

    def moments(n, carry):
        decay = rate[pl.ds(n, 1), :]
        sum0 = jnp.zeros((8, cols), f32)
        sum1 = jnp.zeros((8, cols), f32)
        for r in range(0, seq, ROWS):
            where = (lax.broadcasted_iota(jnp.int32, (ROWS, cols), 0) + r).astype(f32) / seq
            term = jnp.exp(-decay * where) * gf[r : r + ROWS]
            sum0 = sum0 + fold(term)
            sum1 = sum1 + fold(term * where)
        m0 = jnp.sum(sum0, axis=0, keepdims=True)
        m1 = jnp.sum(sum1, axis=0, keepdims=True)
        size = jnp.sqrt(2.0 * decay / seq)
        o_res[pl.ds(n, 1), :] = size * m0 / norm
        o_rate[pl.ds(n, 1), :] = res[pl.ds(n, 1), :] * size * (0.5 * m0 - decay * m1) / norm
        return carry

    lax.fori_loop(0, order_n, moments, 0)

    def weight(zs):
        o_weight[span(zs, cols), :] = dot(mbuf[zs], gbuf[z]) * (1.0 / norm)

    weight(z)
    line_step(2, mixed_block, s_m, r_m)
    for d in hops:
        weight(ring(z, d))
    for group in (c_o, c_s):
        for d in order:
            group[d].wait_recv()
    own.wait()
    own_short.wait()
    line_end(gm_block, s_g, r_g)
    line_end(mixed_block, s_m, r_m)
    for zs in range(peers):
        for where in range(3):
            gm_out(zs, where).wait_send()
    for group in (c_p, c_w, c_wf, c_o, c_s):
        for key in group:
            group[key].wait_send()


def body(projections, short_taps, residues, decay_rates, skip_gain, grad_mixed, out_weight):
    tokens, _, width = projections.shape
    peers = lax.axis_size("ctx")
    seq = tokens * peers
    if seq > 1024 or peers != 4 or lax.axis_size("ch") != 4 or lax.axis_size("groups") != 2:
        return body_factored(
            projections, short_taps, residues, decay_rates, skip_gain, grad_mixed, out_weight
        )
    cols = width // peers
    wide = grad_mixed.shape[1]
    f32, bf16 = jnp.float32, jnp.bfloat16
    taps = lax.dynamic_slice_in_dim(short_taps, lax.axis_index("ctx") * cols, cols, 2)
    taps = taps.reshape(SHORT * 3, cols)
    tables = jnp.asarray(wave_tables(seq))
    order = residues.shape[1]
    vmem = pl.BlockSpec(memory_space=pltpu.VMEM)
    any_ = pl.BlockSpec(memory_space=pl.ANY)
    near = peers - 1
    dma = pltpu.SemaphoreType.DMA
    S = jax.ShapeDtypeStruct
    V = pltpu.VMEM
    outs = pl.pallas_call(
        mega,
        out_shape=(
            S((3, tokens, width), bf16), S((16, width), f32), S((1, cols), f32),
            S((order, cols), f32), S((order, cols), f32), S((width, wide), f32),
        ),
        in_specs=[any_, any_, any_] + [vmem] * 5,
        out_specs=[vmem] * 6,
        scratch_shapes=[
            V((3, seq, cols), bf16), V((peers, cols, wide), bf16), V((peers, seq, wide), bf16),
            V((peers, cols, seq), bf16), V((3, seq, cols), bf16), V((16, cols), f32),
            V((2 * seq, seq), bf16), V((2 * seq, seq), bf16), V((seq, 2 * seq), bf16), V((seq, 2 * seq), bf16),
            V((2 * seq, cols), f32), V((2 * seq, cols), f32), V((2 * seq, cols), f32),
            V((2 * seq, cols), bf16), V((2 * seq, cols), bf16), V((seq, cols), bf16), V((seq, cols), bf16),
            V((3, PAD + seq, cols), f32), V((3, seq, cols), f32), V((seq, cols), bf16),
            V((3, seq + PAD, cols), f32), V((seq, cols), f32), V((seq, cols), f32), V((8, cols), f32),
            V((seq, cols), bf16), V((seq, cols), f32),
            dma((5,)), dma((near,)), dma((near,)), dma((2 * near,)), dma((2 * near,)),
            dma((peers * near,)), dma((peers * near,)), dma((near,)), dma((near,)), dma((near,)), dma((near,)),
            dma((2 * near,)), dma((2 * near,)), dma((near,)), dma((near,)), dma((near,)), dma((near,)),
        ],
        compiler_params=pltpu.CompilerParams(
            collective_id=0, has_side_effects=True, vmem_limit_bytes=56 * 1024 * 1024
        ),
    )(
        projections.transpose(1, 0, 2), out_weight, grad_mixed, taps, skip_gain[None],
        residues.T, decay_rates.T, tables,
    )
    grad_proj, short, skip, grad_res, grad_rate, grad_weight = outs
    return (
        grad_proj.transpose(1, 0, 2),
        short[: SHORT * 3].reshape(SHORT, 3, width),
        skip[0],
        grad_res.T,
        grad_rate.T,
        grad_weight,
    )


def solution(mesh):
    return jax.shard_map(
        body,
        mesh=mesh,
        in_specs=(
            P(("groups", "ctx"), None, "ch"),
            P(None, None, "ch"),
            P(("ch", "ctx"), None),
            P(("ch", "ctx"), None),
            P(("ch", "ctx")),
            P(("groups", "ctx"), "ch"),
            P("ch", "ctx"),
        ),
        out_specs=(
            P(("groups", "ctx"), None, "ch"),
            P("groups", None, "ch"),
            P(("groups", "ch", "ctx")),
            P(("groups", "ch", "ctx"), None),
            P(("groups", "ch", "ctx"), None),
            P(("groups", "ch"), "ctx"),
        ),
        check_vma=False,
    )
```

```python
from functools import partial
import math

import jax
import jax.numpy as jnp
import numpy as np
from jax import lax
from jax.experimental import pallas as pl
from jax.experimental.pallas import tpu as pltpu
from jax.sharding import PartitionSpec as P

SHORT = 3


def from_behind(x, axis, by):
    peers = lax.axis_size(axis)
    pairs = [(i, i + by) for i in range(peers) if 0 <= i + by < peers]
    return lax.ppermute(x, axis, pairs)


def make_filter(residues, decay_rates, seq_len):
    positions = jnp.arange(seq_len, dtype=jnp.float32) / seq_len
    amplitude = residues * jnp.sqrt(2.0 * decay_rates / seq_len)
    basis = jnp.exp(-decay_rates[:, :, None] * positions[None, None, :])
    return jnp.einsum("cn,cnt->ct", amplitude, basis, precision=lax.Precision.HIGHEST)


def circle(rows_count, cols_count, period):
    left_idx = jnp.arange(rows_count, dtype=jnp.int32)[:, None]
    right_idx = jnp.arange(cols_count, dtype=jnp.int32)[None, :]
    angle = (left_idx * right_idx % period).astype(jnp.float32) * (2.0 * math.pi / period)
    return (jnp.cos(angle), jnp.sin(angle))


def spectral_tables(length):
    factor_a = 1
    while factor_a * factor_a * 4 <= length and length % (factor_a * 2) == 0:
        factor_a = factor_a * 2
    factor_b = length // factor_a
    a_cos, a_sin = circle(factor_a, factor_a, factor_a)
    b_cos, b_sin = circle(factor_b, factor_b, factor_b)
    t_cos, t_sin = circle(factor_a, factor_b, length)
    return (length, factor_a, factor_b, a_cos, a_sin, b_cos, b_sin, t_cos, t_sin)


def forward_dft(signal, tables):
    length, factor_a, factor_b, a_cos, a_sin, b_cos, b_sin, t_cos, t_sin = tables
    highest = lax.Precision.HIGHEST
    channels, seq_len = signal.shape
    grid = jnp.pad(signal, ((0, 0), (0, length - seq_len))).reshape(channels, factor_a, factor_b)
    part_real = jnp.einsum("ka,cab->ckb", a_cos, grid, precision=highest)
    part_imag = -jnp.einsum("ka,cab->ckb", a_sin, grid, precision=highest)
    turn_real = part_real * t_cos + part_imag * t_sin
    turn_imag = part_imag * t_cos - part_real * t_sin
    out_real = jnp.einsum("ckb,bm->ckm", turn_real, b_cos, precision=highest) + jnp.einsum(
        "ckb,bm->ckm", turn_imag, b_sin, precision=highest
    )
    out_imag = jnp.einsum("ckb,bm->ckm", turn_imag, b_cos, precision=highest) - jnp.einsum(
        "ckb,bm->ckm", turn_real, b_sin, precision=highest
    )
    return (out_real, out_imag)


def inverse_dft(spec_real, spec_imag, seq_len, tables):
    length, factor_a, factor_b, a_cos, a_sin, b_cos, b_sin, t_cos, t_sin = tables
    highest = lax.Precision.HIGHEST
    channels = spec_real.shape[0]
    mid_real = jnp.einsum("ckm,mb->ckb", spec_real, b_cos, precision=highest) - jnp.einsum(
        "ckm,mb->ckb", spec_imag, b_sin, precision=highest
    )
    mid_imag = jnp.einsum("ckm,mb->ckb", spec_imag, b_cos, precision=highest) + jnp.einsum(
        "ckm,mb->ckb", spec_real, b_sin, precision=highest
    )
    turn_real = mid_real * t_cos - mid_imag * t_sin
    turn_imag = mid_imag * t_cos + mid_real * t_sin
    values = jnp.einsum("ak,ckb->cab", a_cos, turn_real, precision=highest) - jnp.einsum(
        "ak,ckb->cab", a_sin, turn_imag, precision=highest
    )
    return values.reshape(channels, length)[:, :seq_len] / length


def short_mix(extended, short_taps, tokens):
    running = jnp.zeros((tokens,) + extended.shape[1:], jnp.float32)
    for lag_index in range(SHORT):
        start_row = SHORT - 1 - lag_index
        running = running + short_taps[lag_index] * extended[start_row : start_row + tokens]
    return running


def mix_long(gate_cols, spec_h, gain, seq_len, tables):
    gate_f = gate_cols.astype(jnp.float32)
    u_real, u_imag = forward_dft(gate_f, tables)
    prod_real = spec_h[0] * u_real - spec_h[1] * u_imag
    prod_imag = spec_h[0] * u_imag + spec_h[1] * u_real
    mix_cols = (inverse_dft(prod_real, prod_imag, seq_len, tables) + gain[:, None] * gate_f).astype(
        jnp.bfloat16
    )
    return (mix_cols, (u_real, u_imag))


def grad_long(grad_cols_in, gate_cols, spec_u, spec_h, gain, seq_len, tables):
    grad_f = grad_cols_in.astype(jnp.float32)
    g_real, g_imag = forward_dft(grad_f, tables)
    back_real = spec_h[0] * g_real + spec_h[1] * g_imag
    back_imag = spec_h[0] * g_imag - spec_h[1] * g_real
    grad_cols = (
        inverse_dft(back_real, back_imag, seq_len, tables) + gain[:, None] * grad_f
    ).astype(jnp.bfloat16)
    corr_real = g_real * spec_u[0] + g_imag * spec_u[1]
    corr_imag = g_imag * spec_u[0] - g_real * spec_u[1]
    grad_filter = inverse_dft(corr_real, corr_imag, seq_len, tables)
    skip_sum = jnp.sum(grad_f * gate_cols.astype(jnp.float32), axis=1)
    return (grad_cols, grad_filter, skip_sum)


def body_factored(projections, short_taps, residues, decay_rates, skip_gain, grad_mixed, out_weight):
    tokens = projections.shape[0]
    seq_len = tokens * lax.axis_size("ctx")
    norm_factor = math.sqrt(seq_len)
    tables = spectral_tables(2 * seq_len)
    earlier = from_behind(projections[tokens - SHORT + 1 :], "ctx", 1)
    ext_proj = jnp.concatenate([earlier, projections], axis=0)
    mixed_in = short_mix(ext_proj, short_taps, tokens)
    query_rows = mixed_in[:, 0]
    key_rows = mixed_in[:, 1]
    value_rows = mixed_in[:, 2]
    gated_rows = (key_rows * value_rows).astype(jnp.bfloat16)
    long_filter, filter_vjp = jax.vjp(partial(make_filter, seq_len=seq_len), residues, decay_rates)
    spec_h = forward_dft(long_filter, tables)
    out_rows = lax.all_gather(grad_mixed, "ch", axis=1, tiled=True)
    grad_out = lax.dot_general(
        out_rows,
        lax.all_gather(out_weight, "ctx", axis=1, tiled=True),
        (((1,), (1,)), ((), ())),
        preferred_element_type=jnp.float32,
    )
    grad_y = (grad_out * query_rows).astype(jnp.bfloat16)
    gate_cols, grad_cols_in = (
        lax.all_to_all(gated_rows.T, "ctx", split_axis=0, concat_axis=1, tiled=True),
        lax.all_to_all(grad_y.T, "ctx", split_axis=0, concat_axis=1, tiled=True),
    )
    mix_cols, spec_u = mix_long(gate_cols, spec_h, skip_gain, seq_len, tables)
    grad_cols, grad_filter, skip_sum = grad_long(
        grad_cols_in, gate_cols, spec_u, spec_h, skip_gain, seq_len, tables
    )
    returned = (
        lax.all_to_all(mix_cols, "ctx", split_axis=1, concat_axis=0, tiled=True),
        lax.all_to_all(grad_cols, "ctx", split_axis=1, concat_axis=0, tiled=True),
    )
    mix_rows = returned[0].T
    grad_gated = returned[1].T
    grad_res, grad_rate = filter_vjp(grad_filter)
    grad_residues = grad_res / norm_factor
    grad_log_rates = grad_rate * decay_rates / norm_factor
    grad_skip = skip_sum / norm_factor
    mixed_out = (query_rows * mix_rows).astype(jnp.bfloat16)
    grad_mix = jnp.stack(
        [grad_out * mix_rows, grad_gated * value_rows, grad_gated * key_rows], axis=1
    )
    later = from_behind(grad_mix[: SHORT - 1], "ctx", -1)
    ext_grad = jnp.concatenate([grad_mix, later], axis=0)
    running = jnp.zeros(grad_mix.shape, jnp.float32)
    short_terms = []
    for lag_index in range(SHORT):
        running = running + short_taps[lag_index] * ext_grad[lag_index : lag_index + tokens]
        start_row = SHORT - 1 - lag_index
        short_terms.append(jnp.sum(grad_mix * ext_proj[start_row : start_row + tokens], axis=0))
    grad_projections = running.astype(jnp.bfloat16)
    grad_short = lax.psum(jnp.stack(short_terms, axis=0), "ctx") / norm_factor
    partial_term = lax.dot_general(
        mixed_out, out_rows, (((0,), (0,)), ((), ())), preferred_element_type=jnp.float32
    )
    weight_sum = lax.psum_scatter(partial_term, "ctx", scatter_dimension=1, tiled=True)
    grad_weight = weight_sum / norm_factor
    return (grad_projections, grad_short, grad_skip, grad_residues, grad_log_rates, grad_weight)


MESH = pl.DeviceIdType.MESH
FINE = 16
ROWS = 64
PAD = 8


def wave_tables(seq_len):
    odd = np.arange(seq_len, dtype=np.int64)[None, :] * 2 + 1
    steps = np.arange(seq_len, dtype=np.int64)[None, :]
    coarse = np.arange(seq_len // FINE, dtype=np.int64)[:, None] * FINE
    fine = np.arange(FINE, dtype=np.int64)[:, None]
    rows = []
    for product in (2 * coarse * steps, (2 * fine + 1) * steps, coarse * odd, fine * odd):
        angle = (product % (4 * seq_len)) * (2.0 * math.pi / (4 * seq_len))
        rows += [np.cos(angle), np.sin(angle)]
    return np.concatenate(rows, axis=0).astype(np.float32)


def dot(a, b):
    return lax.dot_general(a, b, (((1,), (0,)), ((), ())), preferred_element_type=jnp.float32)


def mega(
    proj, w, gm, taps, gain, res, rate, tab,
    o_proj, o_short, o_skip, o_res, o_rate, mbuf, o_gm,
    pbuf, wbuf, gbuf, gp, short_own,
    wh, wl, th, tl, pq, ab, de, sp_h, sp_l, x_h, x_l,
    pf, qkv, gated, gmix, gout, mix, filt, gy, gf,
    loc, s_p, r_p, s_g, r_g, s_gf, r_gf, s_w, r_w, s_wf, r_wf, s_m, r_m, s_o, r_o, s_s, r_s,
):
    f32, bf16 = jnp.float32, jnp.bfloat16
    peers = lax.axis_size("ctx")
    tokens, cols = proj.shape[1], proj.shape[2] // peers
    seq = tokens * peers
    wide = gm.shape[1]
    half = cols // 2
    z = lax.axis_index("ctx")
    k = lax.axis_index("ch")
    g = lax.axis_index("groups")
    norm = math.sqrt(seq)
    hops = range(1, peers)

    def ring(i, d):
        return lax.rem(i + d + peers, peers)

    def span(i, n):
        return pl.ds(pl.multiple_of(i * n, n), n)

    barrier = pltpu.get_barrier_semaphore()
    for d in hops:
        pl.semaphore_signal(barrier, inc=1, device_id={"ctx": ring(z, d)}, device_id_type=MESH)
        pl.semaphore_signal(barrier, inc=1, device_id={"ch": ring(k, d)}, device_id_type=MESH)
    pl.semaphore_signal(barrier, inc=1, device_id={"groups": 1 - g}, device_id_type=MESH)

    def remote(src, dst, ssem, rsem, **where):
        return pltpu.make_async_remote_copy(
            src_ref=src, dst_ref=dst, send_sem=ssem, recv_sem=rsem,
            device_id=where, device_id_type=MESH,
        )

    local = [
        pltpu.make_async_copy(proj.at[:, :, span(z, cols)], pbuf.at[:, span(z, tokens), :], loc.at[0]),
        pltpu.make_async_copy(gm, gbuf.at[k, span(z, tokens), :], loc.at[1]),
        pltpu.make_async_copy(w.at[span(z, cols), :], wbuf.at[z], loc.at[2]),
    ]
    for c in local:
        c.start()
    pl.semaphore_wait(barrier, 2 * (peers - 1) + 1)

    order = (2, 1, 3)
    c_p, c_w, c_wf = {}, {}, {}
    mate = k + 1 - 2 * lax.rem(k, 2)
    across = lax.rem(k + 2, 4)

    def line(i, side, block, ssem, rsem):
        slot = block(ring(z, -side * i))
        sem = i if side > 0 else peers - 1 + i
        return remote(slot, slot, ssem.at[sem], rsem.at[sem], ctx=ring(z, side))

    def line_sends(i, side):
        return (z + 1 < peers) & (z >= i) if side > 0 else (z >= 1) & (z + i < peers)

    def line_gets(i, side):
        return z >= i + 1 if side > 0 else z + i + 1 < peers

    def line_start(i, block, ssem, rsem):
        for side in (1, -1):
            @pl.when(line_sends(i, side))
            def _():
                line(i, side, block, ssem, rsem).start()

    def line_step(i, block, ssem, rsem, then=None):
        for side in (1, -1):
            @pl.when(line_gets(i, side))
            def _():
                line(i, side, block, ssem, rsem).wait_recv()
                if then is not None:
                    then(ring(z, -side * (i + 1)))
        if i + 1 < peers - 1:
            line_start(i + 1, block, ssem, rsem)

    def line_end(block, ssem, rsem):
        for i in range(peers - 1):
            for side in (1, -1):
                @pl.when(line_sends(i, side))
                def _():
                    line(i, side, block, ssem, rsem).wait_send()

    def gm_block(zs):
        return gbuf.at[k, span(zs, tokens), :]

    def gm_out(zs, where):
        n = zs + peers * where
        column = (k, k, across)[where]
        part = gbuf.at[column, span(zs, tokens), :]
        return remote(part, part, s_gf.at[n], r_gf.at[n], ch=(mate, across, mate)[where])

    def gm_spread(zs):
        gm_out(zs, 1).start()
        gm_out(zs, 0).start()

    def mixed_block(zs):
        return mbuf.at[zs]

    local[1].wait()
    line_start(0, gm_block, s_g, r_g)
    gm_spread(z)
    for d in order:
        zp = ring(z, d)
        c_p[d] = remote(proj.at[:, :, span(zp, cols)], pbuf.at[:, span(z, tokens), :], s_p.at[d - 1], r_p.at[d - 1], ctx=zp)
        c_p[d].start()
    groups_of = seq // FINE
    at = [0]
    for n in (groups_of, groups_of, FINE, FINE, groups_of, groups_of, FINE, FINE):
        at.append(at[-1] + n)

    def put(high, low, rows, columns, x):
        top = x.astype(bf16)
        high[rows, columns] = top
        low[rows, columns] = (x - top.astype(f32)).astype(bf16)

    def fill(i, carry):
        for base, high, low, by_row in ((0, wh, wl, True), (4, th, tl, False)):
            ca, sa = tab[pl.ds(at[base] + i, 1), :], tab[pl.ds(at[base + 1] + i, 1), :]
            cb, sb = tab[at[base + 2] : at[base + 3], :], tab[at[base + 3] : at[base + 4], :]
            cos, sin = ca * cb - sa * sb, sa * cb + ca * sb
            first = pl.multiple_of(i * FINE, FINE)
            if by_row:
                put(high, low, pl.ds(first, FINE), slice(None), cos)
                put(high, low, pl.ds(pl.multiple_of(seq + i * FINE, FINE), FINE), slice(None), sin)
            else:
                put(high, low, pl.ds(first, FINE), slice(0, seq), cos)
                put(high, low, pl.ds(first, FINE), slice(seq, 2 * seq), sin)
        return carry

    lax.fori_loop(0, groups_of, fill, 0)
    line_step(0, gm_block, s_g, r_g, gm_spread)

    order_n = res.shape[0]
    amp = jnp.sqrt(2.0 * rate[...] / seq)
    scaled = res[...] * amp
    for r in range(0, seq, ROWS):
        where = (lax.broadcasted_iota(jnp.int32, (ROWS, cols), 0) + r).astype(f32) / seq
        total = jnp.zeros((ROWS, cols), f32)
        for n in range(order_n):
            total = total + scaled[n : n + 1] * jnp.exp(-rate[n : n + 1, :] * where)
        put(x_h, x_l, slice(r, r + ROWS), slice(None), total)
    line_step(1, gm_block, s_g, r_g, gm_spread)
    block = 256
    for r in range(0, 2 * seq, block):
        rows = slice(r, r + block)
        pq[rows] = dot(wh[rows], x_h[...]) + dot(wl[rows], x_h[...]) + dot(wh[rows], x_l[...])

    line_step(2, gm_block, s_g, r_g, gm_spread)

    def spectrum(out, x):
        for r in range(0, 2 * seq, block):
            rows = slice(r, r + block)
            out[rows] = dot(wh[rows], x[...]) + dot(wl[rows], x[...])

    def product(x, y, conj):
        for r in range(0, seq, ROWS):
            lo, hi = slice(r, r + ROWS), slice(seq + r, seq + r + ROWS)
            a, b, c, d = x[lo], x[hi], y[lo], y[hi]
            if conj:
                put(sp_h, sp_l, lo, slice(None), a * c + b * d)
                put(sp_h, sp_l, hi, slice(None), a * d - b * c)
            else:
                put(sp_h, sp_l, lo, slice(None), a * c - b * d)
                put(sp_h, sp_l, hi, slice(None), a * d + b * c)

    def inverse(r, n):
        rows = slice(r, r + n)
        total = dot(th[rows], sp_h[...]) + dot(tl[rows], sp_h[...]) + dot(th[rows], sp_l[...])
        return total * (1.0 / seq)

    for i in range(3):
        pf[i, 0:PAD] = jnp.zeros((PAD, cols), f32)
        gmix[i, seq : seq + PAD] = jnp.zeros((PAD, cols), f32)
    gain_row = gain[...]

    for d in order:
        c_p[d].wait_send()
    for d in order:
        zp = ring(z, d)
        c_w[d] = remote(
            w.at[pl.ds(pl.multiple_of(zp * cols + g * half, half), half), :],
            wbuf.at[z, span(g, half), :], s_w.at[d - 1], r_w.at[d - 1], ctx=zp,
        )
        c_w[d].start()
    local[0].wait()
    for d in order:
        c_p[d].wait_recv()
    for r in range(0, seq, ROWS):
        for i in range(3):
            pf[i, PAD + r : PAD + r + ROWS] = pbuf[i, r : r + ROWS].astype(f32)
        for i in range(3):
            total = jnp.zeros((ROWS, cols), f32)
            for j in range(SHORT):
                total = total + taps[3 * j + i : 3 * j + i + 1] * pf[i, PAD + r - j : PAD + r - j + ROWS]
            qkv[i, r : r + ROWS] = total
        gated[r : r + ROWS] = (qkv[1, r : r + ROWS] * qkv[2, r : r + ROWS]).astype(bf16)
    spectrum(ab, gated)
    product(pq, ab, False)
    for r in range(0, seq, block):
        rows = slice(r, r + block)
        m = (inverse(r, block) + gain_row * gated[rows].astype(f32)).astype(bf16).astype(f32)
        mix[rows] = m
        mbuf[z, :, rows] = (qkv[0, rows] * m).T.astype(bf16)

    line_start(0, mixed_block, s_m, r_m)
    local[2].wait()
    for zs in range(peers):
        gm_out(zs, 1).wait_recv()
        gm_out(zs, 2).start()
    for d in order:
        c_w[d].wait_recv()
        part = wbuf.at[ring(z, -d), span(g, half), :]
        c_wf[d] = remote(part, part, s_wf.at[d - 1], r_wf.at[d - 1], groups=1 - g)
        c_wf[d].start()
    line_step(0, mixed_block, s_m, r_m)
    for zs in range(peers):
        gm_out(zs, 0).wait_recv()
        gm_out(zs, 2).wait_recv()
    for d in order:
        c_wf[d].wait_recv()

    keep = pltpu.make_async_copy(gbuf.at[z], o_gm, loc.at[3])
    keep.start()
    for r in range(0, seq, block):
        rows = slice(r, r + block)
        total = jnp.zeros((block, cols), f32)
        for j in range(peers):
            total = total + lax.dot_general(
                gbuf[j, rows, :], wbuf[j], (((1,), (1,)), ((), ())), preferred_element_type=f32
            )
        gout[rows] = total
    for r in range(0, seq, ROWS):
        rows = slice(r, r + ROWS)
        go = gout[rows]
        gy[rows] = (go * qkv[0, rows]).astype(bf16)
        gmix[0, rows] = go * mix[rows]
    c_o, c_s, own = {}, {}, {}

    def send_gradient(i):
        for r in range(0, seq, ROWS):
            total = jnp.zeros((ROWS, cols), f32)
            for j in range(SHORT):
                total = total + taps[3 * j + i : 3 * j + i + 1] * gmix[i, r + j : r + j + ROWS]
            gp[i, r : r + ROWS] = total.astype(bf16)
        for d in order:
            zp = ring(z, d)
            n = i * (peers - 1) + d - 1
            c_o[i, d] = remote(gp.at[i, span(zp, tokens), :], o_proj.at[i, :, span(z, cols)], s_o.at[n], r_o.at[n], ctx=zp)
            c_o[i, d].start()
        own[i] = pltpu.make_async_copy(gp.at[i, span(z, tokens), :], o_proj.at[i, :, span(z, cols)], loc.at[5 + i])
        own[i].start()

    send_gradient(0)
    spectrum(de, gy)
    product(pq, de, True)
    line_step(1, mixed_block, s_m, r_m)
    for r in range(0, seq, block):
        rows = slice(r, r + block)
        gg = (inverse(r, block) + gain_row * gy[rows].astype(f32)).astype(bf16).astype(f32)
        gmix[1, rows] = gg * qkv[2, rows]
        gmix[2, rows] = gg * qkv[1, rows]
    for i in (1, 2):
        send_gradient(i)

    def fold(x):
        return jnp.sum(x.reshape(ROWS // 8, 8, cols), axis=0)

    for i in range(3):
        sums = [jnp.zeros((8, cols), f32) for _ in range(SHORT)]
        for r in range(0, seq, ROWS):
            here = gmix[i, r : r + ROWS]
            for j in range(SHORT):
                sums[j] = sums[j] + fold(here * pf[i, PAD + r - j : PAD + r - j + ROWS])
        for j in range(SHORT):
            short_own[3 * j + i : 3 * j + i + 1, :] = jnp.sum(sums[j], axis=0, keepdims=True) / norm
    for j in range(9, 16):
        short_own[j : j + 1, :] = jnp.zeros((1, cols), f32)
    for d in order:
        c_s[d] = remote(short_own, o_short.at[:, span(z, cols)], s_s.at[d - 1], r_s.at[d - 1], ctx=ring(z, d))
        c_s[d].start()
    own_short = pltpu.make_async_copy(short_own, o_short.at[:, span(z, cols)], loc.at[4])
    own_short.start()
    skip = jnp.zeros((8, cols), f32)
    for r in range(0, seq, ROWS):
        rows = slice(r, r + ROWS)
        skip = skip + fold(gy[rows].astype(f32) * gated[rows].astype(f32))
    o_skip[...] = jnp.sum(skip, axis=0, keepdims=True) / norm
    product(ab, de, True)
    for r in range(0, seq, block):
        gf[r : r + block] = inverse(r, block)

    def moments(n, carry):
        decay = rate[pl.ds(n, 1), :]
        sum0 = jnp.zeros((8, cols), f32)
        sum1 = jnp.zeros((8, cols), f32)
        for r in range(0, seq, ROWS):
            where = (lax.broadcasted_iota(jnp.int32, (ROWS, cols), 0) + r).astype(f32) / seq
            term = jnp.exp(-decay * where) * gf[r : r + ROWS]
            sum0 = sum0 + fold(term)
            sum1 = sum1 + fold(term * where)
        m0 = jnp.sum(sum0, axis=0, keepdims=True)
        m1 = jnp.sum(sum1, axis=0, keepdims=True)
        size = jnp.sqrt(2.0 * decay / seq)
        o_res[pl.ds(n, 1), :] = size * m0 / norm
        o_rate[pl.ds(n, 1), :] = res[pl.ds(n, 1), :] * size * (0.5 * m0 - decay * m1) / norm
        return carry

    lax.fori_loop(0, order_n, moments, 0)

    line_step(2, mixed_block, s_m, r_m)
    keep.wait()
    for group in (c_o, c_s):
        for key in group:
            group[key].wait_recv()
    for i in own:
        own[i].wait()
    own_short.wait()
    line_end(gm_block, s_g, r_g)
    line_end(mixed_block, s_m, r_m)
    for zs in range(peers):
        for where in range(3):
            gm_out(zs, where).wait_send()
    for group in (c_w, c_wf, c_o, c_s):
        for key in group:
            group[key].wait_send()


def finish(mixed, gm, rows, short, skip, res, rate, o_weight, o_rows, o_short, o_skip, o_res, o_rate):
    o_weight[...] = dot(mixed[0], gm[...]) * (1.0 / math.sqrt(gm.shape[0]))
    o_rows[...] = rows[...]
    for j in range(SHORT):
        o_short[j] = short[3 * j : 3 * j + 3]
    o_skip[...] = skip[...]
    o_res[...] = res[...]
    o_rate[...] = rate[...]


def body(projections, short_taps, residues, decay_rates, skip_gain, grad_mixed, out_weight):
    tokens, _, width = projections.shape
    peers = lax.axis_size("ctx")
    seq = tokens * peers
    if seq > 1024 or peers != 4 or lax.axis_size("ch") != 4 or lax.axis_size("groups") != 2:
        return body_factored(
            projections, short_taps, residues, decay_rates, skip_gain, grad_mixed, out_weight
        )
    cols = width // peers
    wide = grad_mixed.shape[1]
    f32, bf16 = jnp.float32, jnp.bfloat16
    taps = lax.dynamic_slice_in_dim(short_taps, lax.axis_index("ctx") * cols, cols, 2)
    taps = taps.reshape(SHORT * 3, cols)
    tables = jnp.asarray(wave_tables(seq))
    order = residues.shape[1]
    vmem = pl.BlockSpec(memory_space=pltpu.VMEM)
    any_ = pl.BlockSpec(memory_space=pl.ANY)
    near = peers - 1
    dma = pltpu.SemaphoreType.DMA
    S = jax.ShapeDtypeStruct
    V = pltpu.VMEM
    outs = pl.pallas_call(
        mega,
        out_shape=(
            S((3, tokens, width), bf16), S((16, width), f32), S((1, cols), f32),
            S((order, cols), f32), S((order, cols), f32),
            S((peers, cols, seq), bf16), S((seq, wide), bf16),
        ),
        in_specs=[any_, any_, any_] + [vmem] * 5,
        out_specs=[vmem] * 7,
        scratch_shapes=[
            V((3, seq, cols), bf16), V((peers, cols, wide), bf16), V((peers, seq, wide), bf16),
            V((3, seq, cols), bf16), V((16, cols), f32),
            V((2 * seq, seq), bf16), V((2 * seq, seq), bf16), V((seq, 2 * seq), bf16), V((seq, 2 * seq), bf16),
            V((2 * seq, cols), f32), V((2 * seq, cols), f32), V((2 * seq, cols), f32),
            V((2 * seq, cols), bf16), V((2 * seq, cols), bf16), V((seq, cols), bf16), V((seq, cols), bf16),
            V((3, PAD + seq, cols), f32), V((3, seq, cols), f32), V((seq, cols), bf16),
            V((3, seq + PAD, cols), f32), V((seq, cols), f32), V((seq, cols), f32), V((8, cols), f32),
            V((seq, cols), bf16), V((seq, cols), f32),
            dma((8,)), dma((near,)), dma((near,)), dma((2 * near,)), dma((2 * near,)),
            dma((peers * near,)), dma((peers * near,)), dma((near,)), dma((near,)), dma((near,)), dma((near,)),
            dma((2 * near,)), dma((2 * near,)), dma((3 * near,)), dma((3 * near,)), dma((near,)), dma((near,)),
        ],
        compiler_params=pltpu.CompilerParams(
            collective_id=0, has_side_effects=True, vmem_limit_bytes=56 * 1024 * 1024
        ),
    )(
        projections.transpose(1, 0, 2), out_weight, grad_mixed, taps, skip_gain[None],
        residues.T, decay_rates.T, tables,
    )
    proj_rows, short, skip, grad_res, grad_rate, mixed, gm_own = outs

    def whole(shape):
        return pl.BlockSpec(shape, lambda i: (0,) * len(shape))

    rows_spec = pl.BlockSpec((3, tokens, cols), lambda i: (0, 0, i))
    grad_weight, grad_proj, grad_short, grad_skip, grad_res, grad_rate = pl.pallas_call(
        finish,
        grid=(peers,),
        out_shape=(
            S((width, wide), f32), S((3, tokens, width), bf16), S((SHORT, 3, width), f32),
            S((1, cols), f32), S((order, cols), f32), S((order, cols), f32),
        ),
        in_specs=[
            pl.BlockSpec((1, cols, seq), lambda i: (i, 0, 0)), whole((seq, wide)), rows_spec,
            pl.BlockSpec((16, cols), lambda i: (0, i)), whole((1, cols)), whole((order, cols)), whole((order, cols)),
        ],
        out_specs=[
            pl.BlockSpec((cols, wide), lambda i: (i, 0)), rows_spec,
            pl.BlockSpec((SHORT, 3, cols), lambda i: (0, 0, i)),
            whole((1, cols)), whole((order, cols)), whole((order, cols)),
        ],
    )(mixed, gm_own, proj_rows, short, skip, grad_res, grad_rate)
    return (
        grad_proj.transpose(1, 0, 2),
        grad_short,
        grad_skip[0],
        grad_res.T,
        grad_rate.T,
        grad_weight,
    )


def solution(mesh):
    return jax.shard_map(
        body,
        mesh=mesh,
        in_specs=(
            P(("groups", "ctx"), None, "ch"),
            P(None, None, "ch"),
            P(("ch", "ctx"), None),
            P(("ch", "ctx"), None),
            P(("ch", "ctx")),
            P(("groups", "ctx"), "ch"),
            P("ch", "ctx"),
        ),
        out_specs=(
            P(("groups", "ctx"), None, "ch"),
            P("groups", None, "ch"),
            P(("groups", "ch", "ctx")),
            P(("groups", "ch", "ctx"), None),
            P(("groups", "ch", "ctx"), None),
            P(("groups", "ch"), "ctx"),
        ),
        check_vma=False,
    )
```
